512 devices in a mesh: gx: 16 (over z_hi, y), gy: 8 (over z_lo, core), gz: 4 (over x).
Axes of the slice: x: 4, y: 4, z: 16 (z_hi: 4, z_lo: 4; z = z_hi * 4 + z_lo), core: 2. Of those that a mesh axis runs over, the one named last changes fastest.
Arguments:
- traces: bfloat16 [8192, 32], P('gx'), may hold values from -6 to 6
- receiver_cell: int32 [8192], P('gx'), may hold values from 0 to 32767
- weight_class: int32 [8192], P('gx'), may hold values from 0 to 15
- weight_table: float32 [16], replicated, may hold values from 0.5 to 2
- obstacle_top: int32 [32, 256], P('gx', 'gy'), may hold values from 128 to 255
- obstacle_thick: int32 [32, 256], P('gx', 'gy'), may hold values from 0 to 128
- courant: float32 [64, 512, 512], P('gx', 'gy', 'gz'), may hold values from 0.06 to 0.25
- p_now: float32 [64, 512, 512], P('gx', 'gy', 'gz'), may hold values from -6 to 6
- p_prev: float32 [64, 512, 512], P('gx', 'gy', 'gz'), may hold values from -6 to 6
Outputs:
- wavefield: float32 [64, 512, 512], P('gx', 'gy', 'gz')
The draws below stay inside these ranges and needn't reach their ends.
All inputs are finite; a program needn't handle non-finite values.
Results may differ from the reference program's by a relative error of at most 0.0003.
Values may be sent and summed in bfloat16 or wider, within the bound.
No kernel may reach another device: no remote copies, remote signals or barrier semaphores. Data moves between devices by JAX's collectives and lax.ppermute only.
A program may use at most 64 MiB of HBM per device.

```python
import math
import jax
import jax.numpy as jnp
from jax import lax

STEPS = 32
NW = 16
NX = 64
NY = 512
NZ = 512
NREC = 8192


def touch_ends(array, rng, smallest, high):
    dims = array.shape
    spot = [jax.random.randint(jax.random.fold_in(rng, axis), (), 0, dims[axis]) for axis in range(len(dims))]
    array = array.at[tuple(spot)].set(smallest)
    longest = dims.index(max(dims))
    spot[longest] = (spot[longest] + 1) % dims[longest]
    return array.at[tuple(spot)].set(high)


def steps_of(own_key, dims, split, low, high):
    factor_of = 1.0
    for axis_at, blocks in split:
        steps = jax.random.uniform(jax.random.fold_in(jax.random.fold_in(own_key, 6), axis_at), (blocks,), jnp.float32, low / len(split), high / len(split))
        factor_of = factor_of * jnp.repeat(jnp.exp(steps), dims[axis_at] // blocks).reshape((-1,) + (1,) * (len(dims) - 1 - axis_at))
    return factor_of


def scatter_about(key, dims, deviation, reach, shards=(), kind=jnp.bfloat16):
    array = deviation * jax.random.normal(key, dims, jnp.float32)
    if shards:
        array = array * steps_of(key, dims, shards, -0.22, 0.18)
    return jnp.clip(array, -reach, reach).astype(kind)


def setup_inputs(seed: int = 0) -> dict:
    streams_of = jax.random.split(jax.random.key(seed), 10)
    traces = scatter_about(streams_of[0], (NREC, STEPS), 1.0, 6.0, ((0, 16),))
    receiver_cell = touch_ends(jax.random.randint(streams_of[1], (NREC,), 0, NX * NY), jax.random.fold_in(streams_of[1], 1), 0, (NX * NY) - 1).astype(jnp.int32)
    weight_class = touch_ends(jax.random.randint(streams_of[2], (NREC,), 0, NW), jax.random.fold_in(streams_of[2], 1), 0, NW - 1).astype(jnp.int32)
    weight_table = jnp.clip(jnp.exp(jax.random.uniform(streams_of[3], (NW,), jnp.float32, math.log(0.5), math.log(2.0))), 0.5, 2.0)
    obstacle_top = touch_ends(jax.random.randint(streams_of[4], (NX // 2, NY // 2), NZ // 4, NZ // 2), jax.random.fold_in(streams_of[4], 1), NZ // 4, (NZ // 2) - 1).astype(jnp.int32)
    obstacle_thick = touch_ends(jax.random.randint(streams_of[5], (NX // 2, NY // 2), 0, NZ // 4 + 1), jax.random.fold_in(streams_of[5], 1), 0, (NZ // 4 + 1) - 1).astype(jnp.int32)
    courant = jnp.clip(jnp.exp(math.log(0.25) - 1.4271164 * jax.random.uniform(streams_of[6], (NX, NY, NZ), jnp.float32) ** steps_of(streams_of[6], (NX, NY, NZ), ((0, 16), (1, 8), (2, 4)), -0.2, 0.2)), 0.06, 0.25)
    p_now = scatter_about(streams_of[7], (NX, NY, NZ), 1.0, 6.0, ((0, 16), (1, 8), (2, 4)), jnp.float32)
    p_prev = scatter_about(streams_of[8], (NX, NY, NZ), 1.0, 6.0, ((0, 16), (1, 8), (2, 4)), jnp.float32)
    return {"traces": traces, "receiver_cell": receiver_cell, "weight_class": weight_class, "weight_table": weight_table, "obstacle_top": obstacle_top, "obstacle_thick": obstacle_thick, "courant": courant, "p_now": p_now, "p_prev": p_prev}


def laplace_zero(wavefield):
    padded = jnp.pad(wavefield, 1)
    beside_all = padded[2:, 1:-1, 1:-1] + padded[:-2, 1:-1, 1:-1]
    beside_all = beside_all + padded[1:-1, 2:, 1:-1] + padded[1:-1, :-2, 1:-1]
    beside_all = beside_all + padded[1:-1, 1:-1, 2:] + padded[1:-1, 1:-1, :-2]
    return beside_all - 6.0 * wavefield


def reference(traces, receiver_cell, weight_class, weight_table, obstacle_top, obstacle_thick, courant, p_now, p_prev):
    weights = weight_table[weight_class]
    contrib = weights[:, None] * traces.astype(jnp.float32)
    sources = jax.ops.segment_sum(contrib, receiver_cell, num_segments=NX * NY).reshape(NX, NY, STEPS)
    roof = jnp.repeat(jnp.repeat(obstacle_top, 2, axis=0), 2, axis=1)[:, :, None]
    thickness = jnp.repeat(jnp.repeat(obstacle_thick, 2, axis=0), 2, axis=1)[:, :, None]
    depth_cells = jnp.arange(NZ, dtype=jnp.int32)[None, None, :]
    solid = (depth_cells >= roof) & (depth_cells < roof + thickness)
    living = jnp.where(solid, 0.0, 1.0).astype(jnp.float32)
    surface = (jnp.arange(NZ, dtype=jnp.int32) == 0).astype(jnp.float32)

    def advance(counter, carried):
        current, previous = carried
        source_plane = lax.dynamic_index_in_dim(sources, STEPS - 1 - counter, 2, keepdims=False)
        updated = 2.0 * current - previous + courant * laplace_zero(current) + source_plane[:, :, None] * surface
        return (living * updated, current)

    current, previous = lax.fori_loop(0, STEPS, advance, (p_now, p_prev))
    return current
```

```python
import jax
import jax.numpy as jnp
from jax import lax
from jax.experimental import pallas as pl
from jax.experimental.pallas import tpu as pltpu
from jax.sharding import Mesh, PartitionSpec as P


AXES = ("zh", "yc", "zl", "core", "gz")
SIZES = (4, 4, 4, 2, 4)
F32 = jnp.float32
VM = pl.BlockSpec(memory_space=pltpu.VMEM)
SM = pl.BlockSpec(memory_space=pltpu.SMEM)

TY, TZ, KS = 16, 32, 8
PAIRS, WZ, Z0 = 16, 96, 24
UNROLL = 2
FIELD_ROWS, MSG_ROWS = 48, 88


def linear(zh, yc, zl, core, gz):
    return (((zh * 4 + yc) * 4 + zl) * 2 + core) * 4 + gz


def tile_devices():
    table = {}
    for zh in range(4):
        for yc in range(4):
            for zl in range(4):
                for core in range(2):
                    for gz in range(4):
                        gy = zl * 2 + core
                        ty = gy * 4 + ((yc - zl) % 4 if core == 0 else (zl - yc) % 4)
                        tz = gz * 4 + (zh if (gz + core) % 2 == 0 else 3 - zh)
                        table[ty, tz] = linear(zh, yc, zl, core, gz)
    return table


def pairs_along(dy, dz):
    table = tile_devices()
    return [
        (table[ty + dy, tz + dz], table[ty, tz])
        for (ty, tz) in sorted(table)
        if (ty + dy, tz + dz) in table
    ]


def source_of(flags, ys, zs):
    zh = zs + flags[2] * (3 - 2 * zs)
    yc = (flags[0] + ys - 2 * flags[1] * ys) & 3
    return zh * 4 + yc


def lane_group(rows):
    return lax.broadcasted_iota(jnp.int32, (rows, 128), 1) // 32


def low_lanes(rows):
    return lax.broadcasted_iota(jnp.int32, (rows, 128), 1) < 64


def pack_kernel(flags, now, prev, speed, receivers, out):
    group = lane_group(16)
    for field, ref in enumerate((now, prev, speed)):
        for x in range(4):
            parts = [ref[x, pl.ds(q, 16, stride=4), :] for q in range(4)]
            for zs in range(4):
                piece = None
                for q in range(4):
                    turn = (32 * (q - zs)) % 128
                    moved = parts[q] if turn == 0 else pltpu.roll(parts[q], turn, 1)
                    piece = moved if piece is None else jnp.where(group == q, moved, piece)
                for ys in range(4):
                    target = source_of(flags, ys, zs)
                    first = field * 16 + x * 4
                    out[target, first : first + 4, :] = piece[4 * ys : 4 * ys + 4]
    rows = receivers[...]
    for target in range(16):
        out[target, FIELD_ROWS:MSG_ROWS, :] = rows


def unpack_kernel(got, tile):
    low = low_lanes(128)
    solids = []
    for j in range(4):
        stack = []
        for field in range(2):
            stack += [got[src, pl.ds(field * 16 + j, 4, stride=4), :] for src in range(16)]
        tile[128 * j : 128 * j + 128, :] = jnp.concatenate(stack, axis=0).T
        speeds = [got[src, pl.ds(32 + j, 4, stride=4), :] for src in range(16)]
        speeds = jnp.concatenate(speeds, axis=0)
        solids.append(jnp.concatenate([speeds, jnp.zeros_like(speeds)], axis=0).T)
    for j in range(2):
        tile[512 + 128 * j : 640 + 128 * j, :] = jnp.where(
            low, solids[j], pltpu.roll(solids[j + 2], 64, 1)
        )


def source_kernel(flags, got, out):
    out[...] = jnp.zeros_like(out)

    @pl.when(flags[0] == 1)
    def _():
        def shard(src, total):
            terms = jnp.concatenate(
                [got[src, FIELD_ROWS + 8 * j : FIELD_ROWS + 8 * j + 8, :] for j in range(4)], axis=1
            )
            cell = jnp.concatenate([got[src, 80 + j : 81 + j, :] for j in range(4)], axis=1)
            cell = cell.astype(jnp.int32)
            cell_x = cell >> 9
            cell_y = (cell & 511) - flags[1]
            upper = terms.astype(jnp.bfloat16).astype(F32)
            lower = terms - upper
            at_x = (lax.broadcasted_iota(jnp.int32, (64, 512), 0) == cell_x).astype(F32)
            at_x = at_x.astype(jnp.bfloat16)
            here = [jnp.broadcast_to(cell_y, (8, 512)) == y for y in range(2 * PAIRS)]
            for part in (upper, lower):
                rows = jnp.concatenate([jnp.where(h, part, 0.0) for h in here], axis=0)
                total = total + lax.dot_general(
                    rows.astype(jnp.bfloat16),
                    at_x,
                    (((1,), (1,)), ((), ())),
                    preferred_element_type=F32,
                )
            return total

        total = lax.fori_loop(0, 16, shard, jnp.zeros((PAIRS * 16, 64), F32))
        total = jnp.concatenate([total[: PAIRS * 8], total[PAIRS * 8 :]], axis=1)
        out[0] = total.reshape(PAIRS, 8, 128)


def swap(rows):
    return pltpu.roll(rows, 64, 1)


def mix(lower, upper):
    return jnp.where(low_lanes(lower.shape[0]), lower, upper)


def load_pair(a, b, i, z, lower, upper):
    at = z + Z0
    a[i + 1, at : at + lower.shape[0], :] = mix(lower, swap(upper))
    b[i + 1, at : at + lower.shape[0], :] = mix(swap(lower), upper)


def lower_of(a, b, i, z, count):
    at = z + Z0
    return mix(a[i + 1, at : at + count, :], swap(b[i + 1, at : at + count, :]))


def upper_of(a, b, i, z, count):
    at = z + Z0
    return mix(swap(a[i + 1, at : at + count, :]), b[i + 1, at : at + count, :])


def left_speeds(i, top, right):
    if i >= 8:
        return right(i - 8)
    rows = top(i % 4)
    return mix(rows if i < 4 else swap(rows), swap(right(8 + i)))


def advance(a, b, k, m, planes, chunk, z_first, z_last, opening=False):
    top = (lax.broadcasted_iota(jnp.int32, (8, 128), 0) == 0).astype(F32)
    lane = lax.broadcasted_iota(jnp.int32, (8, 128), 1) % 64
    first, last = lane == 0, lane == 63
    starts = range(z_first + Z0, z_last + Z0, 8)
    low = low_lanes(8)

    def weigh(i, nothing):
        for at in starts:
            speed = k[i, at : at + 8, :]
            m[i, at : at + 8, :] = jnp.where(speed > 0.0, 2.0 - 6.0 * speed, 0.0)
        return nothing

    lax.fori_loop(0, PAIRS, weigh, 0)

    def drain(field):
        def row(i, nothing):
            for at in starts:
                kept = field[i + 1, at : at + 8, :]
                field[i + 1, at : at + 8, :] = jnp.where(k[i, at : at + 8, :] > 0.0, kept, 0.0)
            return nothing

        lax.fori_loop(0, PAIRS, row, 0)

    def beside(c):
        return jnp.where(first, 0.0, pltpu.roll(c, 1, 1)) + jnp.where(
            last, 0.0, pltpu.roll(c, 127, 1)
        )

    def one(now, old, step):
        for at in starts:
            now[0, at : at + 8, :] = jnp.where(low, 0.0, swap(now[PAIRS, at : at + 8, :]))
            now[PAIRS + 1, at : at + 8, :] = jnp.where(low, swap(now[1, at : at + 8, :]), 0.0)

        def row(i, carried):
            behind, centre, sides = carried
            ahead = tuple(now[i + 2, at : at + 8, :] for at in starts)
            later = tuple(beside(c) for c in ahead)
            for t, at in enumerate(starts):
                c = centre[t]
                around = sides[t] + (ahead[t] + behind[t])
                around = around + (now[i + 1, at - 1 : at + 7, :] + now[i + 1, at + 1 : at + 9, :])
                new = m[i, at : at + 8, :] * c - old[i + 1, at : at + 8, :]
                new = new + k[i, at : at + 8, :] * around
                if at == Z0:
                    new = new + planes[chunk, i, pl.ds(step, 1), :] * top
                old[i + 1, at : at + 8, :] = new
            return centre, ahead, later

        behind = tuple(now[0, at : at + 8, :] for at in starts)
        centre = tuple(now[1, at : at + 8, :] for at in starts)
        lax.fori_loop(0, PAIRS, row, (behind, centre, tuple(beside(c) for c in centre)), unroll=UNROLL)

    def two(pair, nothing):
        one(a, b, 2 * pair)
        if opening:
            pl.when(pair == 0)(lambda: drain(a))
        one(b, a, 2 * pair + 1)
        return nothing

    if opening:
        drain(b)
    lax.fori_loop(0, KS // 2, two, 0)


def clear(a, b, z_first, z_last):
    zero = jnp.zeros((8, 128), F32)
    for ref in (a, b):
        for i in range(PAIRS + 2):
            ref[i, z_first + Z0 - 8 : z_first + Z0, :] = zero
            ref[i, z_last + Z0 : z_last + Z0 + 8, :] = zero


def round_one(tile, from_z, from_y, from_c, planes, state, msg, speeds, sides, a, b, k, m):
    clear(a, b, 0, 64)
    for lower, upper, z in ((tile, from_y, 0), (from_z, from_c, TZ)):
        for y in range(TY):
            rows = slice(y * TZ, y * TZ + TZ)
            load_pair(a, b, y, z, lower[rows, :], upper[rows, :])
        for y in range(8):
            rows = slice(512 + y * TZ, 512 + y * TZ + TZ)
            k[y, z + Z0 : z + Z0 + TZ, :] = mix(lower[rows, :], swap(upper[rows, :]))
            k[y + 8, z + Z0 : z + Z0 + TZ, :] = mix(swap(lower[rows, :]), upper[rows, :])
    advance(a, b, k, m, planes, 0, 0, 64, opening=True)
    for i in range(PAIRS):
        rows = lower_of(a, b, i, 0, 56)
        state[i * 56 : i * 56 + 56, :] = rows
        if i >= 8:
            msg[(i - 8) * 56 : (i - 8) * 56 + 56, :] = rows
    for i in range(8):
        rows = upper_of(a, b, i, 0, 56)
        state[(i + 16) * 56 : (i + 16) * 56 + 56, :] = rows
        msg[(i + 8) * 56 : (i + 8) * 56 + 56, :] = rows
    for y in range(4):
        msg[896 + y * 56 : 952 + y * 56, :] = mix(
            k[8 + y, Z0 : Z0 + 56, :], swap(k[12 + y, Z0 : Z0 + 56, :])
        )
    for i in range(PAIRS):
        speeds[i] = k[i, Z0 : Z0 + 64, :]
        sides[i] = k[i, Z0 + 16 : Z0 + 32, :]


def load_left(flags, state, from_y, a, b, z, count):
    for i in range(PAIRS):
        rows = from_y[i * count : i * count + count, :]
        if i >= 8:
            rows = jnp.where(flags[0] == 1, state[(i - 8) * count : (i - 7) * count, :], rows)
        load_pair(a, b, i, z, rows, state[(i + 8) * count : (i + 9) * count, :])


def round_two(flags, state, from_y, planes, speeds, tile, msg, a, b, k, m):
    clear(a, b, 0, 56)
    load_left(flags, state, from_y, a, b, 0, 56)
    for i in range(PAIRS):
        k[i, Z0 : Z0 + 56, :] = left_speeds(
            i, lambda y: from_y[896 + y * 56 : 952 + y * 56, :], lambda j: speeds[j, 0:56, :]
        )
    advance(a, b, k, m, planes, 1, 0, 56)
    for y in range(TY):
        rows = lower_of(a, b, y + 8, 0, 48) if y < 8 else upper_of(a, b, y - 8, 0, 48)
        tile[y * 48 : y * 48 + 48, :] = rows
        msg[y * 32 : y * 32 + 32, :] = rows[16:48]


def round_three(flags, tile, from_z, from_y, from_c, planes, speeds, sides, state, msg, a, b, k, m):
    clear(a, b, -16, 48)
    for y in range(TY):
        near = []
        for main, side in ((tile, from_z), (from_y, from_c)):
            near.append(
                jnp.where(
                    flags[0] == 1,
                    main[y * 48 : y * 48 + 16, :],
                    side[y * 32 + 16 : y * 32 + 32, :],
                )
            )
        load_pair(
            a, b, y, -16, from_z[y * 32 : y * 32 + 16, :], from_c[y * 32 : y * 32 + 16, :]
        )
        load_pair(a, b, y, 0, *near)
        load_pair(
            a, b, y, 16, tile[y * 48 + 16 : y * 48 + 48, :], from_y[y * 48 + 16 : y * 48 + 48, :]
        )
        k[y, Z0 - 16 : Z0, :] = sides[y]
        k[y, Z0 : Z0 + 48, :] = speeds[y, 0:48, :]
    advance(a, b, k, m, planes, 2, -16, 48)
    for i in range(PAIRS):
        rows = lower_of(a, b, i, -8, 48)
        state[i * 48 : i * 48 + 48, :] = rows
        if i >= 8:
            msg[(i - 8) * 48 : (i - 8) * 48 + 48, :] = rows
    for i in range(8):
        rows = upper_of(a, b, i, -8, 48)
        state[(i + 16) * 48 : (i + 16) * 48 + 48, :] = rows
        msg[(i + 8) * 48 : (i + 8) * 48 + 48, :] = rows
    for y in range(4):
        msg[768 + y * 8 : 776 + y * 8, :] = mix(
            k[8 + y, Z0 - 8 : Z0, :], swap(k[12 + y, Z0 - 8 : Z0, :])
        )


def round_four(flags, state, from_y, planes, speeds, sides, above, out, a, b, k, m):
    clear(a, b, -8, 40)
    load_left(flags, state, from_y, a, b, -8, 48)
    for i in range(PAIRS):
        k[i, Z0 - 8 : Z0, :] = left_speeds(
            i, lambda y: from_y[768 + y * 8 : 776 + y * 8, :], lambda j: sides[j, 8:16, :]
        )
        k[i, Z0 : Z0 + 40, :] = left_speeds(
            i, lambda y: above[896 + y * 56 : 936 + y * 56, :], lambda j: speeds[j, 0:40, :]
        )
    advance(a, b, k, m, planes, 3, -8, 40)
    for j in range(4):
        first = 4 * j + 9 if j < 2 else 4 * j - 7
        turned = jnp.concatenate([a[first + q, Z0 : Z0 + TZ, :] for q in range(4)], axis=0).T
        half = 0 if j < 2 else 64
        for target in range(16):
            at = half + 4 * target
            out[target, 4 * j : 4 * j + 4, :] = turned[at : at + 4]


def deliver_kernel(flags, got, out):
    group = lane_group(16)
    for x in range(4):
        parts = []
        for zs in range(4):
            rows = [
                got[source_of(flags, ys, zs), pl.ds(x, 4, stride=4), :] for ys in range(4)
            ]
            parts.append(jnp.concatenate(rows, axis=0))
        for q in range(4):
            piece = None
            for zs in range(4):
                turn = (32 * (zs - q)) % 128
                moved = parts[zs] if turn == 0 else pltpu.roll(parts[zs], turn, 1)
                piece = moved if piece is None else jnp.where(group == zs, moved, piece)
            out[x, pl.ds(q, 16, stride=4), :] = piece


def call(kernel, outs, *args, flags=None, scratch=False, cost=2_000_000):
    shapes = [jax.ShapeDtypeStruct(s, F32) for s in outs]
    specs = [VM] * len(args)
    if flags is not None:
        args = (flags,) + args
        specs = [SM] + specs
    return pl.pallas_call(
        kernel,
        out_shape=shapes,
        in_specs=specs,
        out_specs=[VM] * len(outs),
        scratch_shapes=(
            [pltpu.VMEM((PAIRS + 2, WZ, 128), F32)] * 2 + [pltpu.VMEM((PAIRS, WZ, 128), F32)] * 2
            if scratch
            else []
        ),
        compiler_params=pltpu.CompilerParams(vmem_limit_bytes=48 * 1024 * 1024),
        cost_estimate=pl.CostEstimate(flops=cost, bytes_accessed=1_000_000, transcendentals=0),
    )(*args)


def local(
    traces,
    receiver_cell,
    weight_class,
    weight_table,
    obstacle_top,
    obstacle_thick,
    courant,
    p_now,
    p_prev,
):
    zh, yc, zl, core, gz = (lax.axis_index(a) for a in AXES)
    gy = zl * 2 + core
    flip_z = (gz + core) % 2
    ty = gy * 4 + jnp.where(core == 0, yc - zl, zl - yc) % 4
    tz = gz * 4 + zh + flip_z * (3 - 2 * zh)
    place = jnp.stack([zl, core, flip_z]).astype(jnp.int32)

    roof = jnp.repeat(jnp.repeat(obstacle_top, 2, axis=0), 2, axis=1)[:, :, None]
    thickness = jnp.repeat(jnp.repeat(obstacle_thick, 2, axis=0), 2, axis=1)[:, :, None]
    depth = gz * 128 + jnp.arange(128, dtype=jnp.int32)[None, None, :]
    solid = (depth >= roof) & (depth < roof + thickness)
    speed = jnp.where(solid, 0.0, courant)

    classes = weight_class[:, None] == jnp.arange(16, dtype=jnp.int32)[None, :]
    weights = jnp.sum(jnp.where(classes, weight_table[None, :], 0.0), axis=1)
    own = lax.dynamic_slice_in_dim(traces, 24 - 8 * gz, 8, axis=1)[:, ::-1]
    terms = weights[:, None] * own.astype(F32)
    terms = terms.reshape(4, 128, 8).transpose(0, 2, 1).reshape(32, 128)
    cells = receiver_cell.astype(F32).reshape(4, 128)
    receivers = jnp.concatenate([terms, cells, jnp.zeros((4, 128), F32)], axis=0)

    (packed,) = call(
        pack_kernel, [(16, MSG_ROWS, 128)], p_now, p_prev, speed, receivers, flags=place
    )
    got = lax.all_to_all(packed, ("zh", "yc"), 0, 0, tiled=True)

    def moved(array, dy, dz):
        return lax.ppermute(array, AXES, pairs_along(dy, dz))


    (tile,) = call(unpack_kernel, [(768, 128)], got)
    from_y = moved(tile, 1, 0)
    from_z = moved(tile, 0, 1)
    works = jnp.stack([(zh == 3 * core), ty * 16 - 8 * (gz % 2)]).astype(jnp.int32)
    (planes,) = call(source_kernel, [(4, PAIRS, 8, 128)], got, flags=works, cost=20_000_000)
    planes = lax.all_to_all(planes, "gz", 0, 0, tiled=True)
    from_c = moved(from_z, 1, 0)
    first_y = (ty == 0).astype(jnp.int32)[None]
    first_z = (tz == 0).astype(jnp.int32)[None]

    state, msg, speeds, sides = call(
        round_one, [(1344, 128), (1120, 128), (PAIRS, 64, 128), (PAIRS, 16, 128)],
        tile, from_z, from_y, from_c, planes, scratch=True,
    )
    above = moved(msg, -1, 0)
    sides = moved(sides, 0, -1)
    tile, msg = call(
        round_two, [(768, 128), (512, 128)],
        state, above, planes, speeds, flags=first_y, scratch=True,
    )
    from_y = moved(tile, 1, 0)
    from_z = moved(msg, 0, -1)
    from_c = moved(from_z, 1, 0)
    state, msg = call(
        round_three, [(1152, 128), (800, 128)],
        tile, from_z, from_y, from_c, planes, speeds, sides, flags=first_z, scratch=True,
    )
    (out,) = call(
        round_four, [(16, 16, 128)],
        state, moved(msg, -1, 0), planes, speeds, sides, above, flags=first_y, scratch=True,
    )
    out = lax.all_to_all(out, ("zh", "yc"), 0, 0, tiled=True)
    (wavefield,) = call(deliver_kernel, [(4, 64, 128)], out, flags=place)
    return wavefield


def solution(mesh):
    fine = Mesh(mesh.devices.reshape(SIZES), AXES)
    gx, gy, gz = ("zh", "yc"), ("zl", "core"), "gz"
    placed = (
        P(gx, None),
        P(gx),
        P(gx),
        P(),
        P(gx, gy),
        P(gx, gy),
        P(gx, gy, gz),
        P(gx, gy, gz),
        P(gx, gy, gz),
    )

    return jax.shard_map(
        local, mesh=fine, in_specs=placed, out_specs=P(gx, gy, gz), check_vma=False
    )
```

```python
import jax
import jax.numpy as jnp
from jax import lax
from jax.experimental import pallas as pl
from jax.experimental.pallas import tpu as pltpu
from jax.sharding import Mesh, PartitionSpec as P


AXES = ("zh", "yc", "zl", "core", "gz")
SIZES = (4, 4, 4, 2, 4)
F32 = jnp.float32
VM = pl.BlockSpec(memory_space=pltpu.VMEM)
SM = pl.BlockSpec(memory_space=pltpu.SMEM)

TY, TZ, KS = 16, 32, 8
PAIRS, WZ, Z0 = 16, 96, 24
UNROLL = 2
FIELD_ROWS, MSG_ROWS = 48, 72


def linear(zh, yc, zl, core, gz):
    return (((zh * 4 + yc) * 4 + zl) * 2 + core) * 4 + gz


def tile_devices():
    table = {}
    for zh in range(4):
        for yc in range(4):
            for zl in range(4):
                for core in range(2):
                    for gz in range(4):
                        gy = zl * 2 + core
                        ty = gy * 4 + ((yc - zl) % 4 if core == 0 else (zl - yc) % 4)
                        tz = gz * 4 + (zh if gz % 2 == 0 else 3 - zh)
                        table[ty, tz] = linear(zh, yc, zl, core, gz)
    return table


def pairs_along(dy, dz):
    table = tile_devices()
    return [
        (table[ty + dy, tz + dz], table[ty, tz])
        for (ty, tz) in sorted(table)
        if (ty + dy, tz + dz) in table
    ]


def source_of(flags, ys, zs):
    zh = zs + flags[2] * (3 - 2 * zs)
    yc = (flags[0] + ys - 2 * flags[1] * ys) & 3
    return zh * 4 + yc


def lane_group(rows):
    return lax.broadcasted_iota(jnp.int32, (rows, 128), 1) // 32


def low_lanes(rows):
    return lax.broadcasted_iota(jnp.int32, (rows, 128), 1) < 64


def pack_kernel(flags, now, prev, speed, receivers, out):
    group = lane_group(16)
    for field, ref in enumerate((now, prev, speed)):
        for x in range(4):
            parts = [ref[x, pl.ds(q, 16, stride=4), :] for q in range(4)]
            for zs in range(4):
                piece = None
                for q in range(4):
                    turn = (32 * (q - zs)) % 128
                    moved = parts[q] if turn == 0 else pltpu.roll(parts[q], turn, 1)
                    piece = moved if piece is None else jnp.where(group == q, moved, piece)
                for ys in range(4):
                    target = source_of(flags, ys, zs)
                    first = field * 16 + x * 4
                    out[target, first : first + 4, :] = piece[4 * ys : 4 * ys + 4]
    rows = receivers[...]
    for target in range(16):
        out[target, FIELD_ROWS:MSG_ROWS, :] = rows


def unpack_kernel(got, tile, near, far):
    low = low_lanes(128)
    solids = []
    for j in range(4):
        stack = []
        for field in range(2):
            stack += [got[src, pl.ds(field * 16 + j, 4, stride=4), :] for src in range(16)]
        tile[128 * j : 128 * j + 128, :] = jnp.concatenate(stack, axis=0).T
        speeds = [got[src, pl.ds(32 + j, 4, stride=4), :] for src in range(16)]
        speeds = jnp.concatenate(speeds, axis=0)
        solids.append(jnp.concatenate([speeds, jnp.zeros_like(speeds)], axis=0).T)
    for j in range(2):
        tile[512 + 128 * j : 640 + 128 * j, :] = jnp.where(
            low, solids[j], pltpu.roll(solids[j + 2], 64, 1)
        )
    for y in range(24):
        near[y * 16 : y * 16 + 16, :] = tile[y * 32 : y * 32 + 16, :]
        far[y * 16 : y * 16 + 16, :] = tile[y * 32 + 16 : y * 32 + 32, :]


def source_kernel(flags, got, out):
    out[...] = jnp.zeros_like(out)

    @pl.when(flags[0] == 1)
    def _():
        offset = lax.broadcasted_iota(jnp.int32, (8, 512), 0) // 4

        def shard(src, totals):
            terms = jnp.concatenate(
                [got[src, FIELD_ROWS + 4 * j : FIELD_ROWS + 4 * j + 4, :] for j in range(4)], axis=1
            )
            terms = jnp.concatenate([terms, terms], axis=0)
            cell = jnp.concatenate([got[src, 64 + j : 65 + j, :] for j in range(4)], axis=1)
            cell = cell.astype(jnp.int32)
            cell_x = cell >> 9
            upper = terms.astype(jnp.bfloat16).astype(F32)
            lower = terms - upper
            at_x = (lax.broadcasted_iota(jnp.int32, (64, 512), 0) == cell_x).astype(F32)
            at_x = at_x.astype(jnp.bfloat16)
            results = []
            for window in range(2):
                cell_y = jnp.broadcast_to((cell & 511) - flags[1 + window], (8, 512)) - offset
                here = [cell_y == 2 * j for j in range(PAIRS)]
                total = totals[window]
                for part in (upper, lower):
                    rows = jnp.concatenate([jnp.where(h, part, 0.0) for h in here], axis=0)
                    total = total + lax.dot_general(
                        rows.astype(jnp.bfloat16),
                        at_x,
                        (((1,), (1,)), ((), ())),
                        preferred_element_type=F32,
                    )
                results.append(total)
            return tuple(results)

        zero = jnp.zeros((PAIRS * 8, 64), F32)
        totals = lax.fori_loop(0, 16, shard, (zero, zero))
        for window in range(2):
            total = totals[window]
            out[4 * window] = jnp.concatenate([total[: PAIRS * 4], total[PAIRS * 4 :]], axis=1)


def swap(rows):
    return pltpu.roll(rows, 64, 1)


def mix(lower, upper):
    return jnp.where(low_lanes(lower.shape[0]), lower, upper)


def load_pair(a, b, i, z, lower, upper):
    at = z + Z0
    a[i + 1, at : at + lower.shape[0], :] = mix(lower, swap(upper))
    b[i + 1, at : at + lower.shape[0], :] = mix(swap(lower), upper)


def lower_of(a, b, i, z, count):
    at = z + Z0
    return mix(a[i + 1, at : at + count, :], swap(b[i + 1, at : at + count, :]))


def upper_of(a, b, i, z, count):
    at = z + Z0
    return mix(swap(a[i + 1, at : at + count, :]), b[i + 1, at : at + count, :])


def left_speeds(i, top, right):
    if i >= 8:
        return right(i - 8)
    rows = top(i % 4)
    return mix(rows if i < 4 else swap(rows), swap(right(8 + i)))


def advance(a, b, k, m, planes, chunk, z_first, z_last, opening=False):
    top = (lax.broadcasted_iota(jnp.int32, (8, 128), 0) == 0).astype(F32)
    lane = lax.broadcasted_iota(jnp.int32, (8, 128), 1) % 64
    first, last = lane == 0, lane == 63
    starts = range(z_first + Z0, z_last + Z0, 8)
    low = low_lanes(8)

    def weigh(i, nothing):
        for at in starts:
            speed = k[i, at : at + 8, :]
            m[i, at : at + 8, :] = jnp.where(speed > 0.0, 2.0 - 6.0 * speed, 0.0)
        return nothing

    lax.fori_loop(0, PAIRS, weigh, 0)

    def drain(field):
        def row(i, nothing):
            for at in starts:
                kept = field[i + 1, at : at + 8, :]
                field[i + 1, at : at + 8, :] = jnp.where(k[i, at : at + 8, :] > 0.0, kept, 0.0)
            return nothing

        lax.fori_loop(0, PAIRS, row, 0)

    def beside(c):
        return jnp.where(first, 0.0, pltpu.roll(c, 1, 1)) + jnp.where(
            last, 0.0, pltpu.roll(c, 127, 1)
        )

    def one(now, old, step):
        for at in starts:
            now[0, at : at + 8, :] = jnp.where(low, 0.0, swap(now[PAIRS, at : at + 8, :]))
            now[PAIRS + 1, at : at + 8, :] = jnp.where(low, swap(now[1, at : at + 8, :]), 0.0)

        def row(i, carried):
            behind, centre, sides = carried
            ahead = tuple(now[i + 2, at : at + 8, :] for at in starts)
            later = tuple(beside(c) for c in ahead)
            for t, at in enumerate(starts):
                c = centre[t]
                around = sides[t] + (ahead[t] + behind[t])
                around = around + (now[i + 1, at - 1 : at + 7, :] + now[i + 1, at + 1 : at + 9, :])
                new = m[i, at : at + 8, :] * c - old[i + 1, at : at + 8, :]
                new = new + k[i, at : at + 8, :] * around
                if at == Z0:
                    new = new + planes[(step >> 2) * 4 + chunk, pl.ds(i * 4 + (step & 3), 1), :] * top
                old[i + 1, at : at + 8, :] = new
            return centre, ahead, later

        behind = tuple(now[0, at : at + 8, :] for at in starts)
        centre = tuple(now[1, at : at + 8, :] for at in starts)
        lax.fori_loop(0, PAIRS, row, (behind, centre, tuple(beside(c) for c in centre)), unroll=UNROLL)

    def two(pair, nothing):
        one(a, b, 2 * pair)
        if opening:
            pl.when(pair == 0)(lambda: drain(a))
        one(b, a, 2 * pair + 1)
        return nothing

    if opening:
        drain(b)
    lax.fori_loop(0, KS // 2, two, 0)


def clear(a, b, z_first, z_last):
    zero = jnp.zeros((8, 128), F32)
    for ref in (a, b):
        for i in range(PAIRS + 2):
            ref[i, z_first + Z0 - 8 : z_first + Z0, :] = zero
            ref[i, z_last + Z0 : z_last + Z0 + 8, :] = zero


def put_out(a, b, state, msg):
    for i in range(PAIRS):
        rows = lower_of(a, b, i, -8, 48)
        state[i * 48 : i * 48 + 48, :] = rows
        if i >= 8:
            msg[(i - 8) * 48 : (i - 8) * 48 + 48, :] = rows
    for i in range(8):
        rows = upper_of(a, b, i, -8, 48)
        state[(i + 16) * 48 : (i + 16) * 48 + 48, :] = rows
        msg[(i + 8) * 48 : (i + 8) * 48 + 48, :] = rows


def load_right(a, b, tile, from_y, edges, from_c):
    for y in range(TY):
        rows = slice(y * TZ, y * TZ + TZ)
        load_pair(a, b, y, 0, tile[rows, :], from_y[rows, :])
        for z, first in ((TZ, 0), (-16, edges.shape[0] // 2)):
            rows = slice(first + y * 16, first + y * 16 + 16)
            load_pair(a, b, y, z, edges[rows, :], from_c[rows, :])


def load_left(flags, state, from_y, a, b):
    for i in range(PAIRS):
        rows = from_y[i * 48 : i * 48 + 48, :]
        if i >= 8:
            rows = jnp.where(flags[0] == 1, state[(i - 8) * 48 : (i - 7) * 48, :], rows)
        load_pair(a, b, i, -8, rows, state[(i + 8) * 48 : (i + 9) * 48, :])


def load_left_speeds(k, speeds, above):
    for i in range(PAIRS):
        k[i, Z0 - 8 : Z0 + 40, :] = left_speeds(
            i, lambda y: above[768 + y * 48 : 816 + y * 48, :], lambda j: speeds[j, 8:56, :]
        )


def round_one(tile, from_y, edges, from_c, planes, state, msg, speeds, a, b, k, m):
    clear(a, b, -16, 48)
    load_right(a, b, tile, from_y, edges, from_c)
    for lower, upper, first, z, count in (
        (tile, from_y, 512, 0, TZ), (edges, from_c, 256, TZ, 16), (edges, from_c, 640, -16, 16)
    ):
        for y in range(8):
            rows = slice(first + y * count, first + y * count + count)
            at = slice(z + Z0, z + Z0 + count)
            k[y, at, :] = mix(lower[rows, :], swap(upper[rows, :]))
            k[y + 8, at, :] = mix(swap(lower[rows, :]), upper[rows, :])
    advance(a, b, k, m, planes, 0, -16, 48, opening=True)
    put_out(a, b, state, msg)
    for y in range(4):
        at = slice(Z0 - 8, Z0 + 40)
        msg[768 + y * 48 : 816 + y * 48, :] = mix(k[8 + y, at, :], swap(k[12 + y, at, :]))
    for i in range(PAIRS):
        speeds[i] = k[i, Z0 - 16 : Z0 + 48, :]


def round_two(flags, state, from_y, planes, speeds, tile, near, far, a, b, k, m):
    clear(a, b, -8, 40)
    load_left(flags, state, from_y, a, b)
    load_left_speeds(k, speeds, from_y)
    advance(a, b, k, m, planes, 1, -8, 40)
    for y in range(TY):
        rows = lower_of(a, b, y + 8, 0, 32) if y < 8 else upper_of(a, b, y - 8, 0, 32)
        tile[y * 32 : y * 32 + 32, :] = rows
        near[y * 16 : y * 16 + 16, :] = rows[:16]
        far[y * 16 : y * 16 + 16, :] = rows[16:]


def round_three(tile, from_y, edges, from_c, planes, speeds, state, msg, a, b, k, m):
    clear(a, b, -16, 48)
    load_right(a, b, tile, from_y, edges, from_c)
    for i in range(PAIRS):
        k[i, Z0 - 16 : Z0 + 48, :] = speeds[i]
    advance(a, b, k, m, planes, 2, -16, 48)
    put_out(a, b, state, msg)


def round_four(flags, state, from_y, planes, speeds, above, out, a, b, k, m):
    clear(a, b, -8, 40)
    load_left(flags, state, from_y, a, b)
    load_left_speeds(k, speeds, above)
    advance(a, b, k, m, planes, 3, -8, 40)
    for j in range(4):
        first = 4 * j + 9 if j < 2 else 4 * j - 7
        turned = jnp.concatenate([a[first + q, Z0 : Z0 + TZ, :] for q in range(4)], axis=0).T
        half = 0 if j < 2 else 64
        for target in range(16):
            at = half + 4 * target
            out[target, 4 * j : 4 * j + 4, :] = turned[at : at + 4]


def deliver_kernel(flags, got, out):
    group = lane_group(16)
    for x in range(4):
        parts = []
        for zs in range(4):
            rows = [
                got[source_of(flags, ys, zs), pl.ds(x, 4, stride=4), :] for ys in range(4)
            ]
            parts.append(jnp.concatenate(rows, axis=0))
        for q in range(4):
            piece = None
            for zs in range(4):
                turn = (32 * (zs - q)) % 128
                moved = parts[zs] if turn == 0 else pltpu.roll(parts[zs], turn, 1)
                piece = moved if piece is None else jnp.where(group == zs, moved, piece)
            out[x, pl.ds(q, 16, stride=4), :] = piece


def call(kernel, outs, *args, flags=None, scratch=False, cost=2_000_000):
    shapes = [jax.ShapeDtypeStruct(s, F32) for s in outs]
    specs = [VM] * len(args)
    if flags is not None:
        args = (flags,) + args
        specs = [SM] + specs
    return pl.pallas_call(
        kernel,
        out_shape=shapes,
        in_specs=specs,
        out_specs=[VM] * len(outs),
        scratch_shapes=(
            [pltpu.VMEM((PAIRS + 2, WZ, 128), F32)] * 2 + [pltpu.VMEM((PAIRS, WZ, 128), F32)] * 2
            if scratch
            else []
        ),
        compiler_params=pltpu.CompilerParams(vmem_limit_bytes=48 * 1024 * 1024),
        cost_estimate=pl.CostEstimate(flops=cost, bytes_accessed=1_000_000, transcendentals=0),
    )(*args)


def local(
    traces,
    receiver_cell,
    weight_class,
    weight_table,
    obstacle_top,
    obstacle_thick,
    courant,
    p_now,
    p_prev,
):
    zh, yc, zl, core, gz = (lax.axis_index(a) for a in AXES)
    gy = zl * 2 + core
    flip_z = gz % 2
    ty = gy * 4 + jnp.where(core == 0, yc - zl, zl - yc) % 4
    place = jnp.stack([zl, core, flip_z]).astype(jnp.int32)

    roof = jnp.repeat(jnp.repeat(obstacle_top, 2, axis=0), 2, axis=1)[:, :, None]
    thickness = jnp.repeat(jnp.repeat(obstacle_thick, 2, axis=0), 2, axis=1)[:, :, None]
    depth = gz * 128 + jnp.arange(128, dtype=jnp.int32)[None, None, :]
    solid = (depth >= roof) & (depth < roof + thickness)
    speed = jnp.where(solid, 0.0, courant)

    classes = weight_class[:, None] == jnp.arange(16, dtype=jnp.int32)[None, :]
    weights = jnp.sum(jnp.where(classes, weight_table[None, :], 0.0), axis=1)
    own = lax.dynamic_slice_in_dim(traces, 28 - 8 * gz - 4 * core, 4, axis=1)[:, ::-1]
    terms = weights[:, None] * own.astype(F32)
    terms = terms.reshape(4, 128, 4).transpose(0, 2, 1).reshape(16, 128)
    cells = receiver_cell.astype(F32).reshape(4, 128)
    receivers = jnp.concatenate([terms, cells, jnp.zeros((4, 128), F32)], axis=0)

    (packed,) = call(
        pack_kernel, [(16, MSG_ROWS, 128)], p_now, p_prev, speed, receivers, flags=place
    )
    got = lax.all_to_all(packed, ("zh", "yc"), 0, 0, tiled=True)

    def moved(array, dy, dz):
        return lax.ppermute(array, AXES, pairs_along(dy, dz))


    def around(near, far):
        after = moved(near, 0, 1)
        before = moved(far, 0, -1)
        edges = jnp.concatenate([after, before], axis=0)
        return edges, moved(edges, 1, 0)

    tile, near, far = call(unpack_kernel, [(768, 128), (384, 128), (384, 128)], got)
    from_y = moved(tile, 1, 0)
    firsts = [
        zl * 128 - 8 * (gz % 2) + 16 * ((yc - zl) % 4),
        zl * 128 - 8 * (gz % 2) + 64 + 16 * ((zl - yc) % 4),
    ]
    works = jnp.stack([zh == 0] + firsts).astype(jnp.int32)
    (planes,) = call(source_kernel, [(8, PAIRS * 4, 128)], got, flags=works, cost=20_000_000)
    planes = lax.all_to_all(planes, ("core", "gz"), 0, 0, tiled=True)
    edges, from_c = around(near, far)
    first_y = (ty == 0).astype(jnp.int32)[None]

    state, msg, speeds = call(
        round_one, [(1152, 128), (960, 128), (PAIRS, 64, 128)],
        tile, from_y, edges, from_c, planes, scratch=True,
    )
    above = moved(msg, -1, 0)
    tile, near, far = call(
        round_two, [(512, 128), (256, 128), (256, 128)],
        state, above, planes, speeds, flags=first_y, scratch=True,
    )
    from_y = moved(tile, 1, 0)
    edges, from_c = around(near, far)
    state, msg = call(
        round_three, [(1152, 128), (768, 128)],
        tile, from_y, edges, from_c, planes, speeds, scratch=True,
    )
    (out,) = call(
        round_four, [(16, 16, 128)],
        state, moved(msg, -1, 0), planes, speeds, above, flags=first_y, scratch=True,
    )
    out = lax.all_to_all(out, ("zh", "yc"), 0, 0, tiled=True)
    (wavefield,) = call(deliver_kernel, [(4, 64, 128)], out, flags=place)
    return wavefield


def solution(mesh):
    fine = Mesh(mesh.devices.reshape(SIZES), AXES)
    gx, gy, gz = ("zh", "yc"), ("zl", "core"), "gz"
    placed = (
        P(gx, None),
        P(gx),
        P(gx),
        P(),
        P(gx, gy),
        P(gx, gy),
        P(gx, gy, gz),
        P(gx, gy, gz),
        P(gx, gy, gz),
    )

    return jax.shard_map(
        local, mesh=fine, in_specs=placed, out_specs=P(gx, gy, gz), check_vma=False
    )
```

```python
import jax
import jax.numpy as jnp
from jax import lax
from jax.experimental import pallas as pl
from jax.experimental.pallas import tpu as pltpu
from jax.sharding import Mesh, PartitionSpec as P


AXES = ("zh", "yc", "zl", "core", "gz")
SIZES = (4, 4, 4, 2, 4)
F32 = jnp.float32
VM = pl.BlockSpec(memory_space=pltpu.VMEM)
SM = pl.BlockSpec(memory_space=pltpu.SMEM)

TZ, KS = 32, 8
ROWS, WZ, Z0 = 16, 80, 24
FIELD_ROWS, MSG_ROWS = 48, 72


def linear(zh, yc, zl, core, gz):
    return (((zh * 4 + yc) * 4 + zl) * 2 + core) * 4 + gz


def tile_devices():
    table = {}
    for zh in range(4):
        for yc in range(4):
            for zl in range(4):
                for core in range(2):
                    for gz in range(4):
                        gy = zl * 2 + core
                        ty = gy * 4 + ((yc - zl) % 4 if core == 0 else (zl - yc) % 4)
                        tz = gz * 4 + (zh if gz % 2 == 0 else 3 - zh)
                        table[ty, tz] = linear(zh, yc, zl, core, gz)
    return table


def pairs_along(dy, dz):
    table = tile_devices()
    return [
        (table[ty + dy, tz + dz], table[ty, tz])
        for (ty, tz) in sorted(table)
        if (ty + dy, tz + dz) in table
    ]


def source_of(flags, ys, zs):
    zh = zs + flags[2] * (3 - 2 * zs)
    yc = (flags[0] + ys - 2 * flags[1] * ys) & 3
    return zh * 4 + yc


def lane_group(rows):
    return lax.broadcasted_iota(jnp.int32, (rows, 128), 1) // 32


def low_lanes(rows):
    return lax.broadcasted_iota(jnp.int32, (rows, 128), 1) < 64


def pack_kernel(flags, now, prev, speed, receivers, out):
    group = lane_group(16)
    for field, ref in enumerate((now, prev, speed)):
        for x in range(4):
            parts = [ref[x, pl.ds(q, 16, stride=4), :] for q in range(4)]
            for zs in range(4):
                piece = None
                for q in range(4):
                    turn = (32 * (q - zs)) % 128
                    moved = parts[q] if turn == 0 else pltpu.roll(parts[q], turn, 1)
                    piece = moved if piece is None else jnp.where(group == q, moved, piece)
                for ys in range(4):
                    target = source_of(flags, ys, zs)
                    first = field * 16 + x * 4
                    out[target, first : first + 4, :] = piece[4 * ys : 4 * ys + 4]
    rows = receivers[...]
    for target in range(16):
        out[target, FIELD_ROWS:MSG_ROWS, :] = rows


def unpack_kernel(got, tile, near, far):
    low = low_lanes(128)
    solids = []
    for p in range(4):
        parts = [
            [got[pl.ds(16 * field + 4 * p + g, 16, stride=MSG_ROWS), :] for g in range(4)]
            for field in range(3)
        ]
        tile[128 * p : 128 * p + 128, :] = jnp.concatenate(parts[0] + parts[1], axis=0).T
        speeds = jnp.concatenate(parts[2], axis=0)
        solids.append(jnp.concatenate([speeds, jnp.zeros_like(speeds)], axis=0).T)
    for j in range(2):
        tile[512 + 128 * j : 640 + 128 * j, :] = jnp.where(
            low, solids[j], pltpu.roll(solids[j + 2], 64, 1)
        )
    for r in range(24):
        near[r * 16 : r * 16 + 16, :] = tile[r * 32 : r * 32 + 16, :]
        far[r * 16 : r * 16 + 16, :] = tile[r * 32 + 16 : r * 32 + 32, :]


def source_kernel(flags, got, out):
    out[...] = jnp.zeros_like(out)

    @pl.when(flags[0] == 1)
    def _():
        offset = lax.broadcasted_iota(jnp.int32, (8, 512), 0) // 4
        lanes = lax.broadcasted_iota(jnp.int32, (128, 512), 0)

        def shard(src, totals):
            base = src * MSG_ROWS
            terms = got[pl.ds(pl.multiple_of(base + FIELD_ROWS, 8), 16), :]
            cell = got[pl.ds(pl.multiple_of(base + 64, 8), 8), :]
            terms = jnp.concatenate([terms[4 * j : 4 * j + 4] for j in range(4)], axis=1)
            terms = jnp.concatenate([terms, terms], axis=0)
            cell = jnp.concatenate([cell[j : j + 1] for j in range(4)], axis=1)
            cell = cell.astype(jnp.int32)
            cell_x = cell >> 9
            upper = terms.astype(jnp.bfloat16).astype(F32)
            lower = terms - upper
            results = []
            for window in range(2):
                cell_y = (cell & 511) - flags[1 + window]
                lane = jnp.where(
                    (cell_y >= 0) & (cell_y < 32), (cell_y >> 2) * 16 + (cell_x >> 2), -1
                )
                at_lane = (lanes == lane).astype(F32).astype(jnp.bfloat16)
                row = jnp.broadcast_to((cell_x & 3) * 4 + (cell_y & 3), (8, 512)) - offset
                here = [row == 2 * j for j in range(ROWS // 2)]
                total = totals[window]
                for part in (upper, lower):
                    rows = jnp.concatenate([jnp.where(h, part, 0.0) for h in here], axis=0)
                    total = total + lax.dot_general(
                        rows.astype(jnp.bfloat16),
                        at_lane,
                        (((1,), (1,)), ((), ())),
                        preferred_element_type=F32,
                    )
                results.append(total)
            return tuple(results)

        zero = jnp.zeros((ROWS * 4, 128), F32)
        totals = lax.fori_loop(0, 16, shard, (zero, zero))
        for window in range(2):
            out[4 * window] = totals[window]


def swap(rows):
    return pltpu.roll(rows, 64, 1)


def mix(lower, upper):
    return jnp.where(low_lanes(lower.shape[0]), lower, upper)


def load_pair(a, b, r, z, lower, upper):
    at = z + Z0
    a[r, at : at + lower.shape[0], :] = mix(lower, swap(upper))
    b[r, at : at + lower.shape[0], :] = mix(swap(lower), upper)


def middle_of(a, b, r, z, count):
    at = slice(z + Z0, z + Z0 + count)
    return mix(pltpu.roll(a[r, at, :], 96, 1), pltpu.roll(b[r, at, :], 32, 1))


def advance(a, b, k, m, planes, chunk, z_first, z_last, opening=False):
    top = (lax.broadcasted_iota(jnp.int32, (8, 128), 0) == 0).astype(F32)
    lane = lax.broadcasted_iota(jnp.int32, (8, 128), 1)
    first_g, first_m, last_m = lane < 16, lane % 16 == 0, lane % 16 == 15
    span = slice(z_first + Z0, z_last + Z0)
    starts = range(z_first + Z0, z_last + Z0, 8)

    def weigh(r, nothing):
        speed = k[r, span, :]
        m[r, span, :] = jnp.where(speed > 0.0, 2.0 - 6.0 * speed, 0.0)
        return nothing

    lax.fori_loop(0, ROWS, weigh, 0)

    def drain(field):
        def row(r, nothing):
            field[r, span, :] = jnp.where(k[r, span, :] > 0.0, field[r, span, :], 0.0)
            return nothing

        lax.fori_loop(0, ROWS, row, 0)

    def one(now, old, step):
        for at in starts:
            here = slice(at, at + 8)
            c = [now[r, here, :] for r in range(ROWS)]
            for i in range(4):
                before = jnp.where(first_m, 0.0, pltpu.roll(c[12 + i], 1, 1))
                after = jnp.where(last_m, 0.0, pltpu.roll(c[i], 127, 1))
                for p in range(4):
                    r = 4 * p + i
                    around = (before if p == 0 else c[r - 4]) + (after if p == 3 else c[r + 4])
                    if i == 0:
                        below = jnp.where(first_g, 0.0, pltpu.roll(c[r + 3], 16, 1))
                    else:
                        below = c[r - 1]
                    above = pltpu.roll(c[r - 3], 112, 1) if i == 3 else c[r + 1]
                    around = around + (below + above)
                    around = around + (now[r, at - 1 : at + 7, :] + now[r, at + 1 : at + 9, :])
                    new = m[r, here, :] * c[r] - old[r, here, :] + k[r, here, :] * around
                    if at == Z0:
                        row = planes[(step >> 2) * 4 + chunk, pl.ds(r * 4 + (step & 3), 1), :]
                        new = new + row * top
                    old[r, here, :] = new

    def two(pair, nothing):
        one(a, b, 2 * pair)
        if opening:
            pl.when(pair == 0)(lambda: drain(a))
        one(b, a, 2 * pair + 1)
        return nothing

    if opening:
        drain(b)
    lax.fori_loop(0, KS // 2, two, 0)


def clear(a, b, z_first, z_last):
    zero = jnp.zeros((8, 128), F32)
    for ref in (a, b):
        for r in range(ROWS):
            ref[r, z_first + Z0 - 8 : z_first + Z0, :] = zero
            ref[r, z_last + Z0 : z_last + Z0 + 8, :] = zero


def put_out(a, b, state, msg):
    at = slice(Z0 - 8, Z0 + 40)
    for r in range(ROWS):
        state[r] = a[r, at, :]
        state[ROWS + r] = b[r, at, :]
        msg[r * 48 : r * 48 + 48, :] = middle_of(a, b, r, -8, 48)


def load_right(a, b, tile, from_y, edges, from_c):
    for r in range(ROWS):
        rows = slice(r * TZ, r * TZ + TZ)
        load_pair(a, b, r, 0, tile[rows, :], from_y[rows, :])
        for z, first in ((TZ, 0), (-16, edges.shape[0] // 2)):
            rows = slice(first + r * 16, first + r * 16 + 16)
            load_pair(a, b, r, z, edges[rows, :], from_c[rows, :])


def load_left(flags, state, from_y, a, b):
    lane = lax.broadcasted_iota(jnp.int32, (48, 128), 1)
    given = lane < 64 - 32 * flags[0]
    at = slice(Z0 - 8, Z0 + 40)
    for r in range(ROWS):
        rows = from_y[r * 48 : r * 48 + 48, :]
        a[r, at, :] = jnp.where(given, rows, pltpu.roll(state[r], 32, 1))
        b[r, at, :] = jnp.where(given, swap(rows), pltpu.roll(state[ROWS + r], 32, 1))


def load_left_speeds(k, speeds, above):
    given = lax.broadcasted_iota(jnp.int32, (48, 128), 1) < 32
    for r in range(ROWS):
        j, p = r % 4, r // 4
        rows = above[768 + j * 48 : 816 + j * 48, :]
        rows = rows if p == 0 else pltpu.roll(rows, 128 - 32 * p, 1)
        k[r, Z0 - 8 : Z0 + 40, :] = jnp.where(given, rows, pltpu.roll(speeds[r, 8:56, :], 32, 1))


def round_one(tile, from_y, edges, from_c, planes, state, msg, speeds, a, b, k, m):
    clear(a, b, -16, 48)
    load_right(a, b, tile, from_y, edges, from_c)
    for lower, upper, first, z, count in (
        (tile, from_y, 512, 0, TZ), (edges, from_c, 256, TZ, 16), (edges, from_c, 640, -16, 16)
    ):
        for r in range(8):
            rows = slice(first + r * count, first + r * count + count)
            at = slice(z + Z0, z + Z0 + count)
            k[r, at, :] = mix(lower[rows, :], swap(upper[rows, :]))
            k[r + 8, at, :] = mix(swap(lower[rows, :]), upper[rows, :])
    advance(a, b, k, m, planes, 0, -16, 48, opening=True)
    put_out(a, b, state, msg)
    group = lane_group(48)
    for j in range(4):
        rows = k[4 + j, Z0 - 8 : Z0 + 40, :]
        for p in (0, 2, 3):
            moved = pltpu.roll(k[4 * p + j, Z0 - 8 : Z0 + 40, :], (32 * p - 32) % 128, 1)
            rows = jnp.where(group == p, moved, rows)
        msg[768 + j * 48 : 816 + j * 48, :] = rows
    for r in range(ROWS):
        speeds[r] = k[r, Z0 - 16 : Z0 + 48, :]


def round_two(flags, state, from_y, planes, speeds, tile, near, far, a, b, k, m):
    clear(a, b, -8, 40)
    load_left(flags, state, from_y, a, b)
    load_left_speeds(k, speeds, from_y)
    advance(a, b, k, m, planes, 1, -8, 40)
    for r in range(ROWS):
        rows = middle_of(a, b, r, 0, 32)
        tile[r * 32 : r * 32 + 32, :] = rows
        near[r * 16 : r * 16 + 16, :] = rows[:16]
        far[r * 16 : r * 16 + 16, :] = rows[16:]


def round_three(tile, from_y, edges, from_c, planes, speeds, state, msg, a, b, k, m):
    clear(a, b, -16, 48)
    load_right(a, b, tile, from_y, edges, from_c)
    for r in range(ROWS):
        k[r, Z0 - 16 : Z0 + 48, :] = speeds[r]
    advance(a, b, k, m, planes, 2, -16, 48)
    put_out(a, b, state, msg)


def round_four(flags, state, from_y, planes, speeds, above, out, a, b, k, m):
    clear(a, b, -8, 40)
    load_left(flags, state, from_y, a, b)
    load_left_speeds(k, speeds, above)
    advance(a, b, k, m, planes, 3, -8, 40)
    for p in range(4):
        turned = jnp.concatenate([a[4 * p + q, Z0 : Z0 + TZ, :] for q in range(4)], axis=0).T
        for g in range(4):
            out[pl.ds(4 * g + p, 16, stride=16), :] = turned[32 + 16 * g : 48 + 16 * g]


def deliver_kernel(flags, got, out):
    group = lane_group(16)
    for x in range(4):
        parts = []
        for zs in range(4):
            rows = [
                got[source_of(flags, ys, zs), pl.ds(x, 4, stride=4), :] for ys in range(4)
            ]
            parts.append(jnp.concatenate(rows, axis=0))
        for q in range(4):
            piece = None
            for zs in range(4):
                turn = (32 * (zs - q)) % 128
                moved = parts[zs] if turn == 0 else pltpu.roll(parts[zs], turn, 1)
                piece = moved if piece is None else jnp.where(group == zs, moved, piece)
            out[x, pl.ds(q, 16, stride=4), :] = piece


def call(kernel, outs, *args, flags=None, scratch=False, cost=2_000_000):
    shapes = [jax.ShapeDtypeStruct(s, F32) for s in outs]
    specs = [VM] * len(args)
    if flags is not None:
        args = (flags,) + args
        specs = [SM] + specs
    return pl.pallas_call(
        kernel,
        out_shape=shapes,
        in_specs=specs,
        out_specs=[VM] * len(outs),
        scratch_shapes=[pltpu.VMEM((ROWS, WZ, 128), F32)] * 4 if scratch else [],
        compiler_params=pltpu.CompilerParams(vmem_limit_bytes=48 * 1024 * 1024),
        cost_estimate=pl.CostEstimate(flops=cost, bytes_accessed=1_000_000, transcendentals=0),
    )(*args)


def local(
    traces,
    receiver_cell,
    weight_class,
    weight_table,
    obstacle_top,
    obstacle_thick,
    courant,
    p_now,
    p_prev,
):
    zh, yc, zl, core, gz = (lax.axis_index(a) for a in AXES)
    gy = zl * 2 + core
    flip_z = gz % 2
    ty = gy * 4 + jnp.where(core == 0, yc - zl, zl - yc) % 4
    place = jnp.stack([zl, core, flip_z]).astype(jnp.int32)

    roof = jnp.repeat(jnp.repeat(obstacle_top, 2, axis=0), 2, axis=1)[:, :, None]
    thickness = jnp.repeat(jnp.repeat(obstacle_thick, 2, axis=0), 2, axis=1)[:, :, None]
    depth = gz * 128 + jnp.arange(128, dtype=jnp.int32)[None, None, :]
    solid = (depth >= roof) & (depth < roof + thickness)
    speed = jnp.where(solid, 0.0, courant)

    classes = weight_class[:, None] == jnp.arange(16, dtype=jnp.int32)[None, :]
    weights = jnp.sum(jnp.where(classes, weight_table[None, :], 0.0), axis=1)
    own = lax.dynamic_slice_in_dim(traces, 28 - 8 * gz - 4 * core, 4, axis=1)[:, ::-1]
    terms = weights[:, None] * own.astype(F32)
    terms = terms.reshape(4, 128, 4).transpose(0, 2, 1).reshape(16, 128)
    cells = receiver_cell.astype(F32).reshape(4, 128)
    receivers = jnp.concatenate([terms, cells, jnp.zeros((4, 128), F32)], axis=0)

    (packed,) = call(
        pack_kernel, [(16, MSG_ROWS, 128)], p_now, p_prev, speed, receivers, flags=place
    )
    got = lax.all_to_all(packed, ("zh", "yc"), 0, 0, tiled=True).reshape(16 * MSG_ROWS, 128)

    def moved(array, dy, dz):
        return lax.ppermute(array, AXES, pairs_along(dy, dz))


    def around(near, far):
        after = moved(near, 0, 1)
        before = moved(far, 0, -1)
        edges = jnp.concatenate([after, before], axis=0)
        return edges, moved(edges, 1, 0)

    tile, near, far = call(unpack_kernel, [(768, 128), (384, 128), (384, 128)], got)
    from_y = moved(tile, 1, 0)
    firsts = [
        zl * 128 - 8 * (gz % 2) + 16 * ((yc - zl) % 4),
        zl * 128 - 8 * (gz % 2) + 64 + 16 * ((zl - yc) % 4),
    ]
    works = jnp.stack([zh == 0] + firsts).astype(jnp.int32)
    (planes,) = call(source_kernel, [(8, ROWS * 4, 128)], got, flags=works, cost=20_000_000)
    planes = lax.all_to_all(planes, ("core", "gz"), 0, 0, tiled=True)
    edges, from_c = around(near, far)
    first_y = (ty == 0).astype(jnp.int32)[None]

    state, msg, speeds = call(
        round_one, [(2 * ROWS, 48, 128), (960, 128), (ROWS, 64, 128)],
        tile, from_y, edges, from_c, planes, scratch=True,
    )
    above = moved(msg, -1, 0)
    tile, near, far = call(
        round_two, [(512, 128), (256, 128), (256, 128)],
        state, above, planes, speeds, flags=first_y, scratch=True,
    )
    from_y = moved(tile, 1, 0)
    edges, from_c = around(near, far)
    state, msg = call(
        round_three, [(2 * ROWS, 48, 128), (768, 128)],
        tile, from_y, edges, from_c, planes, speeds, scratch=True,
    )
    (out,) = call(
        round_four, [(256, 128)],
        state, moved(msg, -1, 0), planes, speeds, above, flags=first_y, scratch=True,
    )
    out = lax.all_to_all(out.reshape(16, 16, 128), ("zh", "yc"), 0, 0, tiled=True)
    (wavefield,) = call(deliver_kernel, [(4, 64, 128)], out, flags=place)
    return wavefield


def solution(mesh):
    fine = Mesh(mesh.devices.reshape(SIZES), AXES)
    gx, gy, gz = ("zh", "yc"), ("zl", "core"), "gz"
    placed = (
        P(gx, None),
        P(gx),
        P(gx),
        P(),
        P(gx, gy),
        P(gx, gy),
        P(gx, gy, gz),
        P(gx, gy, gz),
        P(gx, gy, gz),
    )

    return jax.shard_map(
        local, mesh=fine, in_specs=placed, out_specs=P(gx, gy, gz), check_vma=False
    )
```

```python
import jax
import jax.numpy as jnp
from jax import lax
from jax.experimental import pallas as pl
from jax.experimental.pallas import tpu as pltpu
from jax.sharding import Mesh, PartitionSpec as P


AXES = ("zh", "yc", "zl", "core", "gz")
SIZES = (4, 4, 4, 2, 4)
F32 = jnp.float32
VM = pl.BlockSpec(memory_space=pltpu.VMEM)
SM = pl.BlockSpec(memory_space=pltpu.SMEM)

TZ, KS = 32, 8
ROWS, WZ, Z0 = 16, 80, 24
FIELD_ROWS, MSG_ROWS = 48, 72


def linear(zh, yc, zl, core, gz):
    return (((zh * 4 + yc) * 4 + zl) * 2 + core) * 4 + gz


def tile_devices():
    table = {}
    for zh in range(4):
        for yc in range(4):
            for zl in range(4):
                for core in range(2):
                    for gz in range(4):
                        gy = zl * 2 + core
                        ty = gy * 4 + ((yc - zl) % 4 if core == 0 else (zl - yc) % 4)
                        tz = gz * 4 + (zh if gz % 2 == 0 else 3 - zh)
                        table[ty, tz] = linear(zh, yc, zl, core, gz)
    return table


def pairs_along(dy, dz):
    table = tile_devices()
    return [
        (table[ty + dy, tz + dz], table[ty, tz])
        for (ty, tz) in sorted(table)
        if (ty + dy, tz + dz) in table
    ]


def source_of(flags, ys, zs):
    zh = zs + flags[2] * (3 - 2 * zs)
    yc = (flags[0] + ys - 2 * flags[1] * ys) & 3
    return zh * 4 + yc


def lane_group(rows):
    return lax.broadcasted_iota(jnp.int32, (rows, 128), 1) // 32


def low_lanes(rows):
    return lax.broadcasted_iota(jnp.int32, (rows, 128), 1) < 64


def pack_kernel(
    flags, table, now, prev, courant, tops, thicks, traces, cells, classes, out, speed, samples
):
    depth = (lax.broadcasted_iota(jnp.int32, (64, 128), 1) + flags[3]).astype(F32)
    row = lax.broadcasted_iota(jnp.int32, (64, 32), 0) // 2
    match = row == lax.broadcasted_iota(jnp.int32, (64, 32), 1)

    def along_y(line):
        values = jnp.where(match, jnp.broadcast_to(line.astype(F32), (64, 32)), 0.0)
        return jnp.broadcast_to(jnp.sum(values, axis=1, keepdims=True), (64, 128))

    for half in range(2):
        roof = along_y(tops[half : half + 1, :])
        floor = roof + along_y(thicks[half : half + 1, :])
        solid = (depth >= roof) & (depth < floor)
        for x in (2 * half, 2 * half + 1):
            speed[x] = jnp.where(solid, 0.0, courant[x])

    given = traces[...].astype(F32)
    for first in range(8):
        samples[first] = given[4 * first : 4 * first + 4, :]
    own = samples[flags[4]]
    kinds = classes[...]
    weights = jnp.zeros((4, 128), F32)
    for kind in range(16):
        weights = jnp.where(kinds == kind, table[kind], weights)
    terms = [own[:, 128 * j : 128 * j + 128] * weights[j : j + 1, :] for j in range(4)]
    receivers = jnp.concatenate(
        terms + [cells[...].astype(F32), jnp.zeros((4, 128), F32)], axis=0
    )
    for target in range(16):
        out[target, FIELD_ROWS:MSG_ROWS, :] = receivers

    group = lane_group(16)
    for field, ref in enumerate((now, prev, speed)):
        for x in range(4):
            parts = [ref[x, pl.ds(q, 16, stride=4), :] for q in range(4)]
            for zs in range(4):
                piece = None
                for q in range(4):
                    turn = (32 * (q - zs)) % 128
                    moved = parts[q] if turn == 0 else pltpu.roll(parts[q], turn, 1)
                    piece = moved if piece is None else jnp.where(group == q, moved, piece)
                for ys in range(4):
                    target = source_of(flags, ys, zs)
                    first = field * 16 + x * 4
                    out[target, first : first + 4, :] = piece[4 * ys : 4 * ys + 4]


def unpack_kernel(got, tile, near, far):
    low = low_lanes(128)
    solids = []
    for p in range(4):
        parts = [
            [got[pl.ds(16 * field + 4 * p + g, 16, stride=MSG_ROWS), :] for g in range(4)]
            for field in range(3)
        ]
        tile[128 * p : 128 * p + 128, :] = jnp.concatenate(parts[0] + parts[1], axis=0).T
        speeds = jnp.concatenate(parts[2], axis=0)
        solids.append(jnp.concatenate([speeds, jnp.zeros_like(speeds)], axis=0).T)
    for j in range(2):
        tile[512 + 128 * j : 640 + 128 * j, :] = jnp.where(
            low, solids[j], pltpu.roll(solids[j + 2], 64, 1)
        )
    for r in range(24):
        near[r * 16 : r * 16 + 16, :] = tile[r * 32 : r * 32 + 16, :]
        far[r * 16 : r * 16 + 16, :] = tile[r * 32 + 16 : r * 32 + 32, :]


def source_kernel(flags, got, out):
    out[...] = jnp.zeros_like(out)

    @pl.when(flags[0] == 1)
    def _():
        offset = lax.broadcasted_iota(jnp.int32, (8, 512), 0) // 4
        lanes = lax.broadcasted_iota(jnp.int32, (128, 512), 0)

        def shard(src, total):
            base = src * MSG_ROWS
            terms = got[pl.ds(pl.multiple_of(base + FIELD_ROWS, 8), 16), :]
            cell = got[pl.ds(pl.multiple_of(base + 64, 8), 8), :]
            terms = jnp.concatenate([terms[4 * j : 4 * j + 4] for j in range(4)], axis=1)
            terms = jnp.concatenate([terms, terms], axis=0)
            cell = jnp.concatenate([cell[j : j + 1] for j in range(4)], axis=1)
            cell = cell.astype(jnp.int32)
            cell_x = cell >> 9
            upper = terms.astype(jnp.bfloat16).astype(F32)
            lower = terms - upper
            at_lane = []
            for window in range(2):
                cell_y = (cell & 511) - flags[1 + window]
                lane = jnp.where(
                    (cell_y >= 0) & (cell_y < 32), (cell_y >> 2) * 16 + (cell_x >> 2), -1
                )
                at_lane.append((lanes == lane).astype(F32))
            at_lane = jnp.concatenate(at_lane, axis=0).astype(jnp.bfloat16)
            row = jnp.broadcast_to((cell_x & 3) * 4 + (cell_y & 3), (8, 512)) - offset
            here = [row == 2 * j for j in range(ROWS // 2)]
            rows = [jnp.where(h, part, 0.0) for part in (upper, lower) for h in here]
            return total + lax.dot_general(
                jnp.concatenate(rows, axis=0).astype(jnp.bfloat16),
                at_lane,
                (((1,), (1,)), ((), ())),
                preferred_element_type=F32,
            )

        total = lax.fori_loop(0, 16, shard, jnp.zeros((ROWS * 8, 256), F32))
        total = total[: ROWS * 4] + total[ROWS * 4 :]
        out[0] = total[:, :128]
        out[4] = total[:, 128:]


def swap(rows):
    return pltpu.roll(rows, 64, 1)


def mix(lower, upper):
    return jnp.where(low_lanes(lower.shape[0]), lower, upper)


def load_pair(a, b, r, z, lower, upper):
    at = z + Z0
    a[r, at : at + lower.shape[0], :] = mix(lower, swap(upper))
    b[r, at : at + lower.shape[0], :] = mix(swap(lower), upper)


def middle_of(a, b, r, z, count):
    at = slice(z + Z0, z + Z0 + count)
    return mix(pltpu.roll(a[r, at, :], 96, 1), pltpu.roll(b[r, at, :], 32, 1))


def advance(a, b, k, m, planes, chunk, z_first, z_last, opening=False):
    top = (lax.broadcasted_iota(jnp.int32, (8, 128), 0) == 0).astype(F32)
    lane = lax.broadcasted_iota(jnp.int32, (8, 128), 1)
    first_g, first_m, last_m = lane < 16, lane % 16 == 0, lane % 16 == 15
    span = slice(z_first + Z0, z_last + Z0)
    starts = range(z_first + Z0, z_last + Z0, 8)

    def weigh(r, nothing):
        speed = k[r, span, :]
        m[r, span, :] = jnp.where(speed > 0.0, 2.0 - 6.0 * speed, 0.0)
        return nothing

    lax.fori_loop(0, ROWS, weigh, 0)

    def drain(field):
        def row(r, nothing):
            field[r, span, :] = jnp.where(k[r, span, :] > 0.0, field[r, span, :], 0.0)
            return nothing

        lax.fori_loop(0, ROWS, row, 0)

    def one(now, old, step):
        for at in starts:
            here = slice(at, at + 8)
            c = [now[r, here, :] for r in range(ROWS)]
            for i in range(4):
                before = jnp.where(first_m, 0.0, pltpu.roll(c[12 + i], 1, 1))
                after = jnp.where(last_m, 0.0, pltpu.roll(c[i], 127, 1))
                for p in range(4):
                    r = 4 * p + i
                    around = (before if p == 0 else c[r - 4]) + (after if p == 3 else c[r + 4])
                    if i == 0:
                        below = jnp.where(first_g, 0.0, pltpu.roll(c[r + 3], 16, 1))
                    else:
                        below = c[r - 1]
                    above = pltpu.roll(c[r - 3], 112, 1) if i == 3 else c[r + 1]
                    around = around + (below + above)
                    around = around + (now[r, at - 1 : at + 7, :] + now[r, at + 1 : at + 9, :])
                    new = m[r, here, :] * c[r] - old[r, here, :] + k[r, here, :] * around
                    if at == Z0:
                        row = planes[(step >> 2) * 4 + chunk, pl.ds(r * 4 + 3 - (step & 3), 1), :]
                        new = new + row * top
                    old[r, here, :] = new

    def two(pair, nothing):
        one(a, b, 2 * pair)
        if opening:
            pl.when(pair == 0)(lambda: drain(a))
        one(b, a, 2 * pair + 1)
        return nothing

    if opening:
        drain(b)
    lax.fori_loop(0, KS // 2, two, 0)


def clear(a, b, z_first, z_last):
    zero = jnp.zeros((8, 128), F32)
    for ref in (a, b):
        for r in range(ROWS):
            ref[r, z_first + Z0 - 8 : z_first + Z0, :] = zero
            ref[r, z_last + Z0 : z_last + Z0 + 8, :] = zero


def put_out(a, b, state, msg):
    at = slice(Z0 - 8, Z0 + 40)
    for r in range(ROWS):
        state[r] = a[r, at, :]
        state[ROWS + r] = b[r, at, :]
        msg[r * 48 : r * 48 + 48, :] = middle_of(a, b, r, -8, 48)


def load_right(a, b, tile, from_y, edges, from_c):
    for r in range(ROWS):
        rows = slice(r * TZ, r * TZ + TZ)
        load_pair(a, b, r, 0, tile[rows, :], from_y[rows, :])
        for z, first in ((TZ, 0), (-16, edges.shape[0] // 2)):
            rows = slice(first + r * 16, first + r * 16 + 16)
            load_pair(a, b, r, z, edges[rows, :], from_c[rows, :])


def load_left(flags, state, from_y, a, b):
    lane = lax.broadcasted_iota(jnp.int32, (48, 128), 1)
    given = lane < 64 - 32 * flags[0]
    at = slice(Z0 - 8, Z0 + 40)
    for r in range(ROWS):
        rows = from_y[r * 48 : r * 48 + 48, :]
        a[r, at, :] = jnp.where(given, rows, pltpu.roll(state[r], 32, 1))
        b[r, at, :] = jnp.where(given, swap(rows), pltpu.roll(state[ROWS + r], 32, 1))


def load_left_speeds(k, speeds, above):
    given = lax.broadcasted_iota(jnp.int32, (48, 128), 1) < 32
    for r in range(ROWS):
        j, p = r % 4, r // 4
        rows = above[768 + j * 48 : 816 + j * 48, :]
        rows = rows if p == 0 else pltpu.roll(rows, 128 - 32 * p, 1)
        k[r, Z0 - 8 : Z0 + 40, :] = jnp.where(given, rows, pltpu.roll(speeds[r, 8:56, :], 32, 1))


def round_one(tile, from_y, edges, from_c, planes, state, msg, speeds, a, b, k, m):
    clear(a, b, -16, 48)
    load_right(a, b, tile, from_y, edges, from_c)
    for lower, upper, first, z, count in (
        (tile, from_y, 512, 0, TZ), (edges, from_c, 256, TZ, 16), (edges, from_c, 640, -16, 16)
    ):
        for r in range(8):
            rows = slice(first + r * count, first + r * count + count)
            at = slice(z + Z0, z + Z0 + count)
            k[r, at, :] = mix(lower[rows, :], swap(upper[rows, :]))
            k[r + 8, at, :] = mix(swap(lower[rows, :]), upper[rows, :])
    advance(a, b, k, m, planes, 0, -16, 48, opening=True)
    put_out(a, b, state, msg)
    group = lane_group(48)
    for j in range(4):
        rows = k[4 + j, Z0 - 8 : Z0 + 40, :]
        for p in (0, 2, 3):
            moved = pltpu.roll(k[4 * p + j, Z0 - 8 : Z0 + 40, :], (32 * p - 32) % 128, 1)
            rows = jnp.where(group == p, moved, rows)
        msg[768 + j * 48 : 816 + j * 48, :] = rows
    for r in range(ROWS):
        speeds[r] = k[r, Z0 - 16 : Z0 + 48, :]


def round_two(flags, state, from_y, planes, speeds, tile, near, far, a, b, k, m):
    clear(a, b, -8, 40)
    load_left(flags, state, from_y, a, b)
    load_left_speeds(k, speeds, from_y)
    advance(a, b, k, m, planes, 1, -8, 40)
    for r in range(ROWS):
        rows = middle_of(a, b, r, 0, 32)
        tile[r * 32 : r * 32 + 32, :] = rows
        near[r * 16 : r * 16 + 16, :] = rows[:16]
        far[r * 16 : r * 16 + 16, :] = rows[16:]


def round_three(tile, from_y, edges, from_c, planes, speeds, state, msg, a, b, k, m):
    clear(a, b, -16, 48)
    load_right(a, b, tile, from_y, edges, from_c)
    for r in range(ROWS):
        k[r, Z0 - 16 : Z0 + 48, :] = speeds[r]
    advance(a, b, k, m, planes, 2, -16, 48)
    put_out(a, b, state, msg)


def round_four(flags, state, from_y, planes, speeds, above, out, a, b, k, m):
    clear(a, b, -8, 40)
    load_left(flags, state, from_y, a, b)
    load_left_speeds(k, speeds, above)
    advance(a, b, k, m, planes, 3, -8, 40)
    for p in range(4):
        turned = jnp.concatenate([a[4 * p + q, Z0 : Z0 + TZ, :] for q in range(4)], axis=0).T
        for g in range(4):
            out[pl.ds(4 * g + p, 16, stride=16), :] = turned[32 + 16 * g : 48 + 16 * g]


def deliver_kernel(flags, got, out):
    group = lane_group(16)
    for x in range(4):
        parts = []
        for zs in range(4):
            rows = [
                got[source_of(flags, ys, zs), pl.ds(x, 4, stride=4), :] for ys in range(4)
            ]
            parts.append(jnp.concatenate(rows, axis=0))
        for q in range(4):
            piece = None
            for zs in range(4):
                turn = (32 * (zs - q)) % 128
                moved = parts[zs] if turn == 0 else pltpu.roll(parts[zs], turn, 1)
                piece = moved if piece is None else jnp.where(group == zs, moved, piece)
            out[x, pl.ds(q, 16, stride=4), :] = piece


def call(kernel, outs, *args, flags=None, scratch=False, cost=2_000_000):
    shapes = [jax.ShapeDtypeStruct(s, F32) for s in outs]
    specs = [VM] * len(args)
    if flags is not None:
        args = (flags,) + args
        specs = [SM] + specs
    return pl.pallas_call(
        kernel,
        out_shape=shapes,
        in_specs=specs,
        out_specs=[VM] * len(outs),
        scratch_shapes=[pltpu.VMEM((ROWS, WZ, 128), F32)] * 4 if scratch else [],
        compiler_params=pltpu.CompilerParams(vmem_limit_bytes=48 * 1024 * 1024),
        cost_estimate=pl.CostEstimate(flops=cost, bytes_accessed=1_000_000, transcendentals=0),
    )(*args)


def local(
    traces,
    receiver_cell,
    weight_class,
    weight_table,
    obstacle_top,
    obstacle_thick,
    courant,
    p_now,
    p_prev,
):
    zh, yc, zl, core, gz = (lax.axis_index(a) for a in AXES)
    gy = zl * 2 + core
    flip_z = gz % 2
    ty = gy * 4 + jnp.where(core == 0, yc - zl, zl - yc) % 4
    place = jnp.stack([zl, core, flip_z, gz * 128, 7 - 2 * gz - core]).astype(jnp.int32)
    packed = pl.pallas_call(
        pack_kernel,
        out_shape=jax.ShapeDtypeStruct((16, MSG_ROWS, 128), F32),
        in_specs=[SM, SM] + [VM] * 8,
        out_specs=VM,
        scratch_shapes=[pltpu.VMEM((4, 64, 128), F32), pltpu.VMEM((8, 4, 512), F32)],
        name="pack",
    )(
        place, weight_table, p_now, p_prev, courant, obstacle_top, obstacle_thick,
        traces.T, receiver_cell.reshape(4, 128), weight_class.reshape(4, 128),
    )
    got = lax.all_to_all(packed, ("zh", "yc"), 0, 0, tiled=True).reshape(16 * MSG_ROWS, 128)

    def moved(array, dy, dz):
        return lax.ppermute(array, AXES, pairs_along(dy, dz))


    def around(near, far):
        after = moved(near, 0, 1)
        before = moved(far, 0, -1)
        edges = jnp.concatenate([after, before], axis=0)
        return edges, moved(edges, 1, 0)

    tile, near, far = call(unpack_kernel, [(768, 128), (384, 128), (384, 128)], got)
    from_y = moved(tile, 1, 0)
    firsts = [
        zl * 128 - 8 * (gz % 2) + 16 * ((yc - zl) % 4),
        zl * 128 - 8 * (gz % 2) + 64 + 16 * ((zl - yc) % 4),
    ]
    works = jnp.stack([zh == 0] + firsts).astype(jnp.int32)
    (planes,) = call(source_kernel, [(8, ROWS * 4, 128)], got, flags=works, cost=20_000_000)
    planes = lax.all_to_all(planes, ("core", "gz"), 0, 0, tiled=True)
    edges, from_c = around(near, far)
    first_y = (ty == 0).astype(jnp.int32)[None]

    state, msg, speeds = call(
        round_one, [(2 * ROWS, 48, 128), (960, 128), (ROWS, 64, 128)],
        tile, from_y, edges, from_c, planes, scratch=True,
    )
    above = moved(msg, -1, 0)
    tile, near, far = call(
        round_two, [(512, 128), (256, 128), (256, 128)],
        state, above, planes, speeds, flags=first_y, scratch=True,
    )
    from_y = moved(tile, 1, 0)
    edges, from_c = around(near, far)
    state, msg = call(
        round_three, [(2 * ROWS, 48, 128), (768, 128)],
        tile, from_y, edges, from_c, planes, speeds, scratch=True,
    )
    (out,) = call(
        round_four, [(256, 128)],
        state, moved(msg, -1, 0), planes, speeds, above, flags=first_y, scratch=True,
    )
    out = lax.all_to_all(out.reshape(16, 16, 128), ("zh", "yc"), 0, 0, tiled=True)
    (wavefield,) = call(deliver_kernel, [(4, 64, 128)], out, flags=place)
    return wavefield


def solution(mesh):
    fine = Mesh(mesh.devices.reshape(SIZES), AXES)
    gx, gy, gz = ("zh", "yc"), ("zl", "core"), "gz"
    placed = (
        P(gx, None),
        P(gx),
        P(gx),
        P(),
        P(gx, gy),
        P(gx, gy),
        P(gx, gy, gz),
        P(gx, gy, gz),
        P(gx, gy, gz),
    )

    return jax.shard_map(
        local, mesh=fine, in_specs=placed, out_specs=P(gx, gy, gz), check_vma=False
    )
```

```python
import jax
import jax.numpy as jnp
from jax import lax
from jax.experimental import pallas as pl
from jax.experimental.pallas import tpu as pltpu
from jax.sharding import Mesh, PartitionSpec as P


AXES = ("zh", "yc", "zl", "core", "gz")
SIZES = (4, 4, 4, 2, 4)
F32 = jnp.float32
VM = pl.BlockSpec(memory_space=pltpu.VMEM)
SM = pl.BlockSpec(memory_space=pltpu.SMEM)

TZ, KS = 32, 8
ROWS, WZ, Z0 = 16, 80, 24
FIELD_ROWS, MSG_ROWS = 48, 72


def linear(zh, yc, zl, core, gz):
    return (((zh * 4 + yc) * 4 + zl) * 2 + core) * 4 + gz


def tile_devices():
    table = {}
    for zh in range(4):
        for yc in range(4):
            for zl in range(4):
                for core in range(2):
                    for gz in range(4):
                        gy = zl * 2 + core
                        ty = gy * 4 + ((yc - zl) % 4 if core == 0 else (zl - yc) % 4)
                        tz = gz * 4 + (zh if gz % 2 == 0 else 3 - zh)
                        table[ty, tz] = linear(zh, yc, zl, core, gz)
    return table


def pairs_along(dy, dz):
    table = tile_devices()
    return [
        (table[ty + dy, tz + dz], table[ty, tz])
        for (ty, tz) in sorted(table)
        if (ty + dy, tz + dz) in table
    ]


def source_of(flags, ys, zs):
    zh = zs + flags[2] * (3 - 2 * zs)
    yc = (flags[0] + ys - 2 * flags[1] * ys) & 3
    return zh * 4 + yc


def lane_group(rows):
    return lax.broadcasted_iota(jnp.int32, (rows, 128), 1) // 32


def low_lanes(rows):
    return lax.broadcasted_iota(jnp.int32, (rows, 128), 1) < 64


def pack_kernel(
    flags, table, now, prev, courant, tops, thicks, traces, cells, classes, out, speed, samples
):
    depth = (lax.broadcasted_iota(jnp.int32, (64, 128), 1) + flags[3]).astype(F32)
    row = lax.broadcasted_iota(jnp.int32, (64, 32), 0) // 2
    match = row == lax.broadcasted_iota(jnp.int32, (64, 32), 1)

    def along_y(line):
        values = jnp.where(match, jnp.broadcast_to(line.astype(F32), (64, 32)), 0.0)
        return jnp.broadcast_to(jnp.sum(values, axis=1, keepdims=True), (64, 128))

    for half in range(2):
        roof = along_y(tops[half : half + 1, :])
        floor = roof + along_y(thicks[half : half + 1, :])
        solid = (depth >= roof) & (depth < floor)
        for x in (2 * half, 2 * half + 1):
            speed[x] = jnp.where(solid, 0.0, courant[x])

    given = traces[...].astype(F32)
    for first in range(8):
        samples[first] = given[4 * first : 4 * first + 4, :]
    own = samples[flags[4]]
    kinds = classes[...]
    weights = jnp.zeros((4, 128), F32)
    for kind in range(16):
        weights = jnp.where(kinds == kind, table[kind], weights)
    terms = [own[:, 128 * j : 128 * j + 128] * weights[j : j + 1, :] for j in range(4)]
    receivers = jnp.concatenate(
        terms + [cells[...].astype(F32), jnp.zeros((4, 128), F32)], axis=0
    )
    for target in range(16):
        out[target, FIELD_ROWS:MSG_ROWS, :] = receivers

    group = lane_group(16)
    for field, ref in enumerate((now, prev, speed)):
        for x in range(4):
            parts = [ref[x, pl.ds(q, 16, stride=4), :] for q in range(4)]
            for zs in range(4):
                piece = None
                for q in range(4):
                    turn = (32 * (q - zs)) % 128
                    moved = parts[q] if turn == 0 else pltpu.roll(parts[q], turn, 1)
                    piece = moved if piece is None else jnp.where(group == q, moved, piece)
                for ys in range(4):
                    target = source_of(flags, ys, zs)
                    first = field * 16 + x * 4
                    out[target, first : first + 4, :] = piece[4 * ys : 4 * ys + 4]


def unpack_kernel(got, tile, near, far):
    low = low_lanes(128)
    solids = []
    for p in range(4):
        parts = [
            [got[pl.ds(16 * field + 4 * p + g, 16, stride=MSG_ROWS), :] for g in range(4)]
            for field in range(3)
        ]
        tile[128 * p : 128 * p + 128, :] = jnp.concatenate(parts[0] + parts[1], axis=0).T
        speeds = jnp.concatenate(parts[2], axis=0)
        solids.append(jnp.concatenate([speeds, jnp.zeros_like(speeds)], axis=0).T)
    for j in range(2):
        tile[512 + 128 * j : 640 + 128 * j, :] = jnp.where(
            low, solids[j], pltpu.roll(solids[j + 2], 64, 1)
        )
    for r in range(24):
        near[r * 16 : r * 16 + 16, :] = tile[r * 32 : r * 32 + 16, :]
        far[r * 16 : r * 16 + 16, :] = tile[r * 32 + 16 : r * 32 + 32, :]


def source_kernel(flags, got, out):
    out[...] = jnp.zeros_like(out)

    @pl.when(flags[0] == 1)
    def _():
        offset = lax.broadcasted_iota(jnp.int32, (8, 512), 0) // 4
        lanes = lax.broadcasted_iota(jnp.int32, (128, 512), 0)

        def shard(src, total):
            base = src * MSG_ROWS
            terms = got[pl.ds(pl.multiple_of(base + FIELD_ROWS, 8), 16), :]
            cell = got[pl.ds(pl.multiple_of(base + 64, 8), 8), :]
            terms = jnp.concatenate([terms[4 * j : 4 * j + 4] for j in range(4)], axis=1)
            terms = jnp.concatenate([terms, terms], axis=0)
            cell = jnp.concatenate([cell[j : j + 1] for j in range(4)], axis=1)
            cell = cell.astype(jnp.int32)
            cell_x = cell >> 9
            upper = terms.astype(jnp.bfloat16).astype(F32)
            lower = terms - upper
            at_lane = []
            for window in range(2):
                cell_y = (cell & 511) - flags[1 + window]
                lane = jnp.where(
                    (cell_y >= 0) & (cell_y < 32), (cell_y >> 2) * 16 + (cell_x >> 2), -1
                )
                at_lane.append((lanes == lane).astype(F32))
            at_lane = jnp.concatenate(at_lane, axis=0).astype(jnp.bfloat16)
            row = jnp.broadcast_to((cell_x & 3) * 4 + (cell_y & 3), (8, 512)) - offset
            here = [row == 2 * j for j in range(ROWS // 2)]
            rows = [jnp.where(h, part, 0.0) for part in (upper, lower) for h in here]
            return total + lax.dot_general(
                jnp.concatenate(rows, axis=0).astype(jnp.bfloat16),
                at_lane,
                (((1,), (1,)), ((), ())),
                preferred_element_type=F32,
            )

        total = lax.fori_loop(0, 16, shard, jnp.zeros((ROWS * 8, 256), F32))
        total = total[: ROWS * 4] + total[ROWS * 4 :]
        out[0] = total[:, :128]
        out[4] = total[:, 128:]


def swap(rows):
    return pltpu.roll(rows, 64, 1)


def mix(lower, upper):
    return jnp.where(low_lanes(lower.shape[0]), lower, upper)


def load_pair(a, b, r, z, lower, upper):
    at = z + Z0
    a[r, at : at + lower.shape[0], :] = mix(lower, swap(upper))
    b[r, at : at + lower.shape[0], :] = mix(swap(lower), upper)


def middle_of(a, b, r, z, count):
    at = slice(z + Z0, z + Z0 + count)
    return mix(pltpu.roll(a[r, at, :], 96, 1), pltpu.roll(b[r, at, :], 32, 1))


def advance(a, b, k, m, planes, chunk, z_first, z_last, opening=False):
    top = (lax.broadcasted_iota(jnp.int32, (8, 128), 0) == 0).astype(F32)
    lane = lax.broadcasted_iota(jnp.int32, (8, 128), 1)
    first_g, first_m, last_m = lane < 16, lane % 16 == 0, lane % 16 == 15
    span = slice(z_first + Z0, z_last + Z0)
    starts = range(z_first + Z0, z_last + Z0, 8)

    def weigh(r, nothing):
        speed = k[r, span, :]
        m[r, span, :] = jnp.where(speed > 0.0, 2.0 - 6.0 * speed, 0.0)
        return nothing

    lax.fori_loop(0, ROWS, weigh, 0)

    def drain(field):
        def row(r, nothing):
            field[r, span, :] = jnp.where(k[r, span, :] > 0.0, field[r, span, :], 0.0)
            return nothing

        lax.fori_loop(0, ROWS, row, 0)

    def one(now, old, step):
        for at in starts:
            here = slice(at, at + 8)
            c = [now[r, here, :] for r in range(ROWS)]
            for i in range(4):
                before = jnp.where(first_m, 0.0, pltpu.roll(c[12 + i], 1, 1))
                after = jnp.where(last_m, 0.0, pltpu.roll(c[i], 127, 1))
                for p in range(4):
                    r = 4 * p + i
                    around = (before if p == 0 else c[r - 4]) + (after if p == 3 else c[r + 4])
                    if i == 0:
                        below = jnp.where(first_g, 0.0, pltpu.roll(c[r + 3], 16, 1))
                    else:
                        below = c[r - 1]
                    above = pltpu.roll(c[r - 3], 112, 1) if i == 3 else c[r + 1]
                    around = around + (below + above)
                    around = around + (now[r, at - 1 : at + 7, :] + now[r, at + 1 : at + 9, :])
                    new = m[r, here, :] * c[r] - old[r, here, :] + k[r, here, :] * around
                    if at == Z0:
                        row = planes[(step >> 2) * 4 + chunk, pl.ds(r * 4 + 3 - (step & 3), 1), :]
                        new = new + row * top
                    old[r, here, :] = new

    def two(pair, nothing):
        one(a, b, 2 * pair)
        if opening:
            pl.when(pair == 0)(lambda: drain(a))
        one(b, a, 2 * pair + 1)
        return nothing

    if opening:
        drain(b)
    lax.fori_loop(0, KS // 2, two, 0)


def clear(a, b, z_first, z_last):
    zero = jnp.zeros((8, 128), F32)
    for ref in (a, b):
        for r in range(ROWS):
            ref[r, z_first + Z0 - 8 : z_first + Z0, :] = zero
            ref[r, z_last + Z0 : z_last + Z0 + 8, :] = zero


def put_out(a, b, state, msg):
    at = slice(Z0 - 8, Z0 + 40)
    for r in range(ROWS):
        state[r] = a[r, at, :]
        state[ROWS + r] = b[r, at, :]
        msg[r * 48 : r * 48 + 48, :] = middle_of(a, b, r, -8, 48)


def load_right(a, b, tile, from_y, edges, corners):
    for r in range(ROWS):
        rows = slice(r * TZ, r * TZ + TZ)
        load_pair(a, b, r, 0, tile[rows, :], from_y[rows, :])
        for z, lower, upper in zip((TZ, -16), edges, corners):
            rows = slice(r * 16, r * 16 + 16)
            load_pair(a, b, r, z, lower[rows, :], upper[rows, :])


def load_left(flags, state, from_y, a, b):
    lane = lax.broadcasted_iota(jnp.int32, (48, 128), 1)
    given = lane < 64 - 32 * flags[0]
    at = slice(Z0 - 8, Z0 + 40)
    for r in range(ROWS):
        rows = from_y[r * 48 : r * 48 + 48, :]
        a[r, at, :] = jnp.where(given, rows, pltpu.roll(state[r], 32, 1))
        b[r, at, :] = jnp.where(given, swap(rows), pltpu.roll(state[ROWS + r], 32, 1))


def load_left_speeds(k, speeds, above):
    given = lax.broadcasted_iota(jnp.int32, (48, 128), 1) < 32
    for r in range(ROWS):
        j, p = r % 4, r // 4
        rows = above[768 + j * 48 : 816 + j * 48, :]
        rows = rows if p == 0 else pltpu.roll(rows, 128 - 32 * p, 1)
        k[r, Z0 - 8 : Z0 + 40, :] = jnp.where(given, rows, pltpu.roll(speeds[r, 8:56, :], 32, 1))


def round_one(tile, from_y, after, before, corner, other, planes, state, msg, speeds, a, b, k, m):
    clear(a, b, -16, 48)
    load_right(a, b, tile, from_y, (after, before), (corner, other))
    for lower, upper, first, z, count in (
        (tile, from_y, 512, 0, TZ), (after, corner, 256, TZ, 16), (before, other, 256, -16, 16)
    ):
        for r in range(8):
            rows = slice(first + r * count, first + r * count + count)
            at = slice(z + Z0, z + Z0 + count)
            k[r, at, :] = mix(lower[rows, :], swap(upper[rows, :]))
            k[r + 8, at, :] = mix(swap(lower[rows, :]), upper[rows, :])
    advance(a, b, k, m, planes, 0, -16, 48, opening=True)
    put_out(a, b, state, msg)
    group = lane_group(48)
    for j in range(4):
        rows = k[4 + j, Z0 - 8 : Z0 + 40, :]
        for p in (0, 2, 3):
            moved = pltpu.roll(k[4 * p + j, Z0 - 8 : Z0 + 40, :], (32 * p - 32) % 128, 1)
            rows = jnp.where(group == p, moved, rows)
        msg[768 + j * 48 : 816 + j * 48, :] = rows
    for r in range(ROWS):
        speeds[r] = k[r, Z0 - 16 : Z0 + 48, :]


def round_two(flags, state, from_y, planes, speeds, tile, near, far, a, b, k, m):
    clear(a, b, -8, 40)
    load_left(flags, state, from_y, a, b)
    load_left_speeds(k, speeds, from_y)
    advance(a, b, k, m, planes, 1, -8, 40)
    for r in range(ROWS):
        rows = middle_of(a, b, r, 0, 32)
        tile[r * 32 : r * 32 + 32, :] = rows
        near[r * 16 : r * 16 + 16, :] = rows[:16]
        far[r * 16 : r * 16 + 16, :] = rows[16:]


def round_three(tile, from_y, after, before, corner, other, planes, speeds, state, msg, a, b, k, m):
    clear(a, b, -16, 48)
    load_right(a, b, tile, from_y, (after, before), (corner, other))
    for r in range(ROWS):
        k[r, Z0 - 16 : Z0 + 48, :] = speeds[r]
    advance(a, b, k, m, planes, 2, -16, 48)
    put_out(a, b, state, msg)


def round_four(flags, state, from_y, planes, speeds, above, out, a, b, k, m):
    clear(a, b, -8, 40)
    load_left(flags, state, from_y, a, b)
    load_left_speeds(k, speeds, above)
    advance(a, b, k, m, planes, 3, -8, 40)
    for p in range(4):
        turned = jnp.concatenate([a[4 * p + q, Z0 : Z0 + TZ, :] for q in range(4)], axis=0).T
        for g in range(4):
            out[pl.ds(4 * g + p, 16, stride=16), :] = turned[32 + 16 * g : 48 + 16 * g]


def deliver_kernel(flags, got, out):
    group = lane_group(16)
    for x in range(4):
        parts = []
        for zs in range(4):
            rows = [
                got[source_of(flags, ys, zs), pl.ds(x, 4, stride=4), :] for ys in range(4)
            ]
            parts.append(jnp.concatenate(rows, axis=0))
        for q in range(4):
            piece = None
            for zs in range(4):
                turn = (32 * (zs - q)) % 128
                moved = parts[zs] if turn == 0 else pltpu.roll(parts[zs], turn, 1)
                piece = moved if piece is None else jnp.where(group == zs, moved, piece)
            out[x, pl.ds(q, 16, stride=4), :] = piece


def call(kernel, outs, *args, flags=None, scratch=False, cost=2_000_000):
    shapes = [jax.ShapeDtypeStruct(s, F32) for s in outs]
    specs = [VM] * len(args)
    if flags is not None:
        args = (flags,) + args
        specs = [SM] + specs
    return pl.pallas_call(
        kernel,
        out_shape=shapes,
        in_specs=specs,
        out_specs=[VM] * len(outs),
        scratch_shapes=[pltpu.VMEM((ROWS, WZ, 128), F32)] * 4 if scratch else [],
        compiler_params=pltpu.CompilerParams(vmem_limit_bytes=48 * 1024 * 1024),
        cost_estimate=pl.CostEstimate(flops=cost, bytes_accessed=1_000_000, transcendentals=0),
    )(*args)


def local(
    traces,
    receiver_cell,
    weight_class,
    weight_table,
    obstacle_top,
    obstacle_thick,
    courant,
    p_now,
    p_prev,
):
    zh, yc, zl, core, gz = (lax.axis_index(a) for a in AXES)
    gy = zl * 2 + core
    flip_z = gz % 2
    ty = gy * 4 + jnp.where(core == 0, yc - zl, zl - yc) % 4
    place = jnp.stack([zl, core, flip_z, gz * 128, 7 - 2 * gz - core]).astype(jnp.int32)
    packed = pl.pallas_call(
        pack_kernel,
        out_shape=jax.ShapeDtypeStruct((16, MSG_ROWS, 128), F32),
        in_specs=[SM, SM] + [VM] * 8,
        out_specs=VM,
        scratch_shapes=[pltpu.VMEM((4, 64, 128), F32), pltpu.VMEM((8, 4, 512), F32)],
        name="pack",
    )(
        place, weight_table, p_now, p_prev, courant, obstacle_top, obstacle_thick,
        traces.T, receiver_cell.reshape(4, 128), weight_class.reshape(4, 128),
    )
    got = lax.all_to_all(packed, ("zh", "yc"), 0, 0, tiled=True).reshape(16 * MSG_ROWS, 128)

    def moved(array, dy, dz):
        return lax.ppermute(array, AXES, pairs_along(dy, dz))


    def around(near, far):
        after = moved(near, 0, 1)
        before = moved(far, 0, -1)
        corner = moved(after, 1, 0)
        other = moved(before, 1, 0)
        return after, before, corner, other

    tile, near, far = call(unpack_kernel, [(768, 128), (384, 128), (384, 128)], got)
    from_y = moved(tile, 1, 0)
    firsts = [
        zl * 128 - 8 * (gz % 2) + 16 * ((yc - zl) % 4),
        zl * 128 - 8 * (gz % 2) + 64 + 16 * ((zl - yc) % 4),
    ]
    works = jnp.stack([zh == 0] + firsts).astype(jnp.int32)
    (planes,) = call(source_kernel, [(8, ROWS * 4, 128)], got, flags=works, cost=20_000_000)
    planes = lax.all_to_all(planes, ("core", "gz"), 0, 0, tiled=True)
    edges = around(near, far)
    first_y = (ty == 0).astype(jnp.int32)[None]

    state, msg, speeds = call(
        round_one, [(2 * ROWS, 48, 128), (960, 128), (ROWS, 64, 128)],
        tile, from_y, *edges, planes, scratch=True,
    )
    above = moved(msg, -1, 0)
    tile, near, far = call(
        round_two, [(512, 128), (256, 128), (256, 128)],
        state, above, planes, speeds, flags=first_y, scratch=True,
    )
    from_y = moved(tile, 1, 0)
    edges = around(near, far)
    state, msg = call(
        round_three, [(2 * ROWS, 48, 128), (768, 128)],
        tile, from_y, *edges, planes, speeds, scratch=True,
    )
    (out,) = call(
        round_four, [(256, 128)],
        state, moved(msg, -1, 0), planes, speeds, above, flags=first_y, scratch=True,
    )
    out = lax.all_to_all(out.reshape(16, 16, 128), ("zh", "yc"), 0, 0, tiled=True)
    (wavefield,) = call(deliver_kernel, [(4, 64, 128)], out, flags=place)
    return wavefield


def solution(mesh):
    fine = Mesh(mesh.devices.reshape(SIZES), AXES)
    gx, gy, gz = ("zh", "yc"), ("zl", "core"), "gz"
    placed = (
        P(gx, None),
        P(gx),
        P(gx),
        P(),
        P(gx, gy),
        P(gx, gy),
        P(gx, gy, gz),
        P(gx, gy, gz),
        P(gx, gy, gz),
    )

    return jax.shard_map(
        local, mesh=fine, in_specs=placed, out_specs=P(gx, gy, gz), check_vma=False
    )
```

```python
import jax
import jax.numpy as jnp
from jax import lax
from jax.experimental import pallas as pl
from jax.experimental.pallas import tpu as pltpu
from jax.sharding import Mesh, PartitionSpec as P


AXES = ("zh", "yc", "zl", "core", "gz")
SIZES = (4, 4, 4, 2, 4)
F32 = jnp.float32
VM = pl.BlockSpec(memory_space=pltpu.VMEM)
SM = pl.BlockSpec(memory_space=pltpu.SMEM)

TZ, KS = 32, 8
ROWS, WZ, Z0 = 16, 80, 24
FIELD_ROWS, MSG_ROWS = 48, 72


def linear(zh, yc, zl, core, gz):
    return (((zh * 4 + yc) * 4 + zl) * 2 + core) * 4 + gz


def tile_devices():
    table = {}
    for zh in range(4):
        for yc in range(4):
            for zl in range(4):
                for core in range(2):
                    for gz in range(4):
                        gy = zl * 2 + core
                        ty = gy * 4 + ((yc - zl) % 4 if core == 0 else (zl - yc) % 4)
                        tz = gz * 4 + (zh if gz % 2 == 0 else 3 - zh)
                        table[ty, tz] = linear(zh, yc, zl, core, gz)
    return table


def pairs_along(dy, dz):
    table = tile_devices()
    return [
        (table[ty + dy, tz + dz], table[ty, tz])
        for (ty, tz) in sorted(table)
        if (ty + dy, tz + dz) in table
    ]


def source_of(flags, ys, zs):
    zh = zs + flags[2] * (3 - 2 * zs)
    yc = (flags[0] + ys - 2 * flags[1] * ys) & 3
    return zh * 4 + yc


def lane_group(rows):
    return lax.broadcasted_iota(jnp.int32, (rows, 128), 1) // 32


def low_lanes(rows):
    return lax.broadcasted_iota(jnp.int32, (rows, 128), 1) < 64


def pack_kernel(
    flags, table, now, prev, courant, tops, thicks, traces, cells, classes, out, speed, samples
):
    depth = (lax.broadcasted_iota(jnp.int32, (64, 128), 1) + flags[3]).astype(F32)
    row = lax.broadcasted_iota(jnp.int32, (64, 32), 0) // 2
    match = row == lax.broadcasted_iota(jnp.int32, (64, 32), 1)

    def along_y(line):
        values = jnp.where(match, jnp.broadcast_to(line.astype(F32), (64, 32)), 0.0)
        return jnp.broadcast_to(jnp.sum(values, axis=1, keepdims=True), (64, 128))

    for half in range(2):
        roof = along_y(tops[half : half + 1, :])
        floor = roof + along_y(thicks[half : half + 1, :])
        solid = (depth >= roof) & (depth < floor)
        for x in (2 * half, 2 * half + 1):
            speed[x] = jnp.where(solid, 0.0, courant[x])

    given = traces[...].astype(F32)
    for first in range(8):
        samples[first] = given[4 * first : 4 * first + 4, :]
    own = samples[flags[4]]
    kinds = classes[...]
    weights = jnp.zeros((4, 128), F32)
    for kind in range(16):
        weights = jnp.where(kinds == kind, table[kind], weights)
    terms = [own[:, 128 * j : 128 * j + 128] * weights[j : j + 1, :] for j in range(4)]
    receivers = jnp.concatenate(
        terms + [cells[...].astype(F32), jnp.zeros((4, 128), F32)], axis=0
    )
    for target in range(16):
        out[target, FIELD_ROWS:MSG_ROWS, :] = receivers

    group = lane_group(16)
    for field, ref in enumerate((now, prev, speed)):
        for x in range(4):
            parts = [ref[x, pl.ds(q, 16, stride=4), :] for q in range(4)]
            for zs in range(4):
                piece = None
                for q in range(4):
                    turn = (32 * (q - zs)) % 128
                    moved = parts[q] if turn == 0 else pltpu.roll(parts[q], turn, 1)
                    piece = moved if piece is None else jnp.where(group == q, moved, piece)
                for ys in range(4):
                    target = source_of(flags, ys, zs)
                    first = field * 16 + x * 4
                    out[target, first : first + 4, :] = piece[4 * ys : 4 * ys + 4]


def unpack_kernel(got, tile, near, far):
    low = low_lanes(128)
    solids = []
    for p in range(4):
        parts = [
            [got[pl.ds(16 * field + 4 * p + g, 16, stride=MSG_ROWS), :] for g in range(4)]
            for field in range(3)
        ]
        tile[128 * p : 128 * p + 128, :] = jnp.concatenate(parts[0] + parts[1], axis=0).T
        speeds = jnp.concatenate(parts[2], axis=0)
        solids.append(jnp.concatenate([speeds, jnp.zeros_like(speeds)], axis=0).T)
    for j in range(2):
        tile[512 + 128 * j : 640 + 128 * j, :] = jnp.where(
            low, solids[j], pltpu.roll(solids[j + 2], 64, 1)
        )
    for r in range(24):
        near[r * 16 : r * 16 + 16, :] = tile[r * 32 : r * 32 + 16, :]
        far[r * 16 : r * 16 + 16, :] = tile[r * 32 + 16 : r * 32 + 32, :]


def source_kernel(flags, got, out, mine, other):
    for ref in (out, mine, other):
        ref[...] = jnp.zeros_like(ref)

    @pl.when(flags[0] == 1)
    def _():
        offset = lax.broadcasted_iota(jnp.int32, (8, 512), 0) // 4
        lanes = lax.broadcasted_iota(jnp.int32, (128, 512), 0)

        def shard(src, total):
            base = src * MSG_ROWS
            terms = got[pl.ds(pl.multiple_of(base + FIELD_ROWS, 8), 16), :]
            cell = got[pl.ds(pl.multiple_of(base + 64, 8), 8), :]
            terms = jnp.concatenate([terms[4 * j : 4 * j + 4] for j in range(4)], axis=1)
            terms = jnp.concatenate([terms, terms], axis=0)
            cell = jnp.concatenate([cell[j : j + 1] for j in range(4)], axis=1)
            cell = cell.astype(jnp.int32)
            cell_x = cell >> 9
            upper = terms.astype(jnp.bfloat16).astype(F32)
            lower = terms - upper
            at_lane = []
            for window in range(2):
                cell_y = (cell & 511) - flags[1 + window]
                lane = jnp.where(
                    (cell_y >= 0) & (cell_y < 32), (cell_y >> 2) * 16 + (cell_x >> 2), -1
                )
                at_lane.append((lanes == lane).astype(F32))
            at_lane = jnp.concatenate(at_lane, axis=0).astype(jnp.bfloat16)
            row = jnp.broadcast_to((cell_x & 3) * 4 + (cell_y & 3), (8, 512)) - offset
            here = [row == 2 * j for j in range(ROWS // 2)]
            rows = [jnp.where(h, part, 0.0) for part in (upper, lower) for h in here]
            return total + lax.dot_general(
                jnp.concatenate(rows, axis=0).astype(jnp.bfloat16),
                at_lane,
                (((1,), (1,)), ((), ())),
                preferred_element_type=F32,
            )

        total = lax.fori_loop(0, 16, shard, jnp.zeros((ROWS * 8, 256), F32))
        total = total[: ROWS * 4] + total[ROWS * 4 :]
        out[4 * flags[3]] = total[:, :128]
        out[4 - 4 * flags[3]] = total[:, 128:]
        mine[...] = total[:, :128]
        other[...] = total[:, 128:]


def swap(rows):
    return pltpu.roll(rows, 64, 1)


def mix(lower, upper):
    return jnp.where(low_lanes(lower.shape[0]), lower, upper)


def load_pair(a, b, r, z, lower, upper):
    at = z + Z0
    a[r, at : at + lower.shape[0], :] = mix(lower, swap(upper))
    b[r, at : at + lower.shape[0], :] = mix(swap(lower), upper)


def middle_of(a, b, r, z, count):
    at = slice(z + Z0, z + Z0 + count)
    return mix(pltpu.roll(a[r, at, :], 96, 1), pltpu.roll(b[r, at, :], 32, 1))


def advance(a, b, k, m, planes, chunk, z_first, z_last, opening=False):
    top = (lax.broadcasted_iota(jnp.int32, (8, 128), 0) == 0).astype(F32)
    lane = lax.broadcasted_iota(jnp.int32, (8, 128), 1)
    first_g, first_m, last_m = lane < 16, lane % 16 == 0, lane % 16 == 15
    span = slice(z_first + Z0, z_last + Z0)
    starts = range(z_first + Z0, z_last + Z0, 8)

    def weigh(r, nothing):
        speed = k[r, span, :]
        m[r, span, :] = jnp.where(speed > 0.0, 2.0 - 6.0 * speed, 0.0)
        return nothing

    lax.fori_loop(0, ROWS, weigh, 0)

    def drain(field):
        def row(r, nothing):
            field[r, span, :] = jnp.where(k[r, span, :] > 0.0, field[r, span, :], 0.0)
            return nothing

        lax.fori_loop(0, ROWS, row, 0)

    def one(now, old, step):
        for at in starts:
            here = slice(at, at + 8)
            c = [now[r, here, :] for r in range(ROWS)]
            for i in range(4):
                before = jnp.where(first_m, 0.0, pltpu.roll(c[12 + i], 1, 1))
                after = jnp.where(last_m, 0.0, pltpu.roll(c[i], 127, 1))
                for p in range(4):
                    r = 4 * p + i
                    around = (before if p == 0 else c[r - 4]) + (after if p == 3 else c[r + 4])
                    if i == 0:
                        below = jnp.where(first_g, 0.0, pltpu.roll(c[r + 3], 16, 1))
                    else:
                        below = c[r - 1]
                    above = pltpu.roll(c[r - 3], 112, 1) if i == 3 else c[r + 1]
                    around = around + (below + above)
                    around = around + (now[r, at - 1 : at + 7, :] + now[r, at + 1 : at + 9, :])
                    new = m[r, here, :] * c[r] - old[r, here, :] + k[r, here, :] * around
                    if at == Z0:
                        row = planes[(step >> 2) * 4 + chunk, pl.ds(r * 4 + 3 - (step & 3), 1), :]
                        new = new + row * top
                    old[r, here, :] = new

    def two(pair, nothing):
        one(a, b, 2 * pair)
        if opening:
            pl.when(pair == 0)(lambda: drain(a))
        one(b, a, 2 * pair + 1)
        return nothing

    if opening:
        drain(b)
    lax.fori_loop(0, KS // 2, two, 0)


def clear(a, b, z_first, z_last):
    zero = jnp.zeros((8, 128), F32)
    for ref in (a, b):
        for r in range(ROWS):
            ref[r, z_first + Z0 - 8 : z_first + Z0, :] = zero
            ref[r, z_last + Z0 : z_last + Z0 + 8, :] = zero


def put_out(a, b, state, msg):
    at = slice(Z0 - 8, Z0 + 40)
    for r in range(ROWS):
        state[r] = a[r, at, :]
        state[ROWS + r] = b[r, at, :]
        msg[r * 48 : r * 48 + 48, :] = middle_of(a, b, r, -8, 48)


def load_right(a, b, tile, from_y, edges, corners):
    for r in range(ROWS):
        rows = slice(r * TZ, r * TZ + TZ)
        load_pair(a, b, r, 0, tile[rows, :], from_y[rows, :])
        for z, lower, upper in zip((TZ, -16), edges, corners):
            rows = slice(r * 16, r * 16 + 16)
            load_pair(a, b, r, z, lower[rows, :], upper[rows, :])


def load_left(flags, state, from_y, a, b):
    lane = lax.broadcasted_iota(jnp.int32, (48, 128), 1)
    given = lane < 64 - 32 * flags[0]
    at = slice(Z0 - 8, Z0 + 40)
    for r in range(ROWS):
        rows = from_y[r * 48 : r * 48 + 48, :]
        a[r, at, :] = jnp.where(given, rows, pltpu.roll(state[r], 32, 1))
        b[r, at, :] = jnp.where(given, swap(rows), pltpu.roll(state[ROWS + r], 32, 1))


def load_left_speeds(k, speeds, above):
    given = lax.broadcasted_iota(jnp.int32, (48, 128), 1) < 32
    for r in range(ROWS):
        j, p = r % 4, r // 4
        rows = above[768 + j * 48 : 816 + j * 48, :]
        rows = rows if p == 0 else pltpu.roll(rows, 128 - 32 * p, 1)
        k[r, Z0 - 8 : Z0 + 40, :] = jnp.where(given, rows, pltpu.roll(speeds[r, 8:56, :], 32, 1))


def round_one(
    flags, tile, from_y, after, before, corner, other, mine, others, state, msg, speeds, a, b, k, m, planes
):
    shown = flags[1].astype(F32)
    planes[4 * flags[0]] = mine[...] * shown
    planes[4 - 4 * flags[0]] = others[...] * shown
    clear(a, b, -16, 48)
    load_right(a, b, tile, from_y, (after, before), (corner, other))
    for lower, upper, first, z, count in (
        (tile, from_y, 512, 0, TZ), (after, corner, 256, TZ, 16), (before, other, 256, -16, 16)
    ):
        for r in range(8):
            rows = slice(first + r * count, first + r * count + count)
            at = slice(z + Z0, z + Z0 + count)
            k[r, at, :] = mix(lower[rows, :], swap(upper[rows, :]))
            k[r + 8, at, :] = mix(swap(lower[rows, :]), upper[rows, :])
    advance(a, b, k, m, planes, 0, -16, 48, opening=True)
    put_out(a, b, state, msg)
    group = lane_group(48)
    for j in range(4):
        rows = k[4 + j, Z0 - 8 : Z0 + 40, :]
        for p in (0, 2, 3):
            moved = pltpu.roll(k[4 * p + j, Z0 - 8 : Z0 + 40, :], (32 * p - 32) % 128, 1)
            rows = jnp.where(group == p, moved, rows)
        msg[768 + j * 48 : 816 + j * 48, :] = rows
    for r in range(ROWS):
        speeds[r] = k[r, Z0 - 16 : Z0 + 48, :]


def round_two(flags, state, from_y, planes, speeds, tile, near, far, a, b, k, m):
    clear(a, b, -8, 40)
    load_left(flags, state, from_y, a, b)
    load_left_speeds(k, speeds, from_y)
    advance(a, b, k, m, planes, 1, -8, 40)
    for r in range(ROWS):
        rows = middle_of(a, b, r, 0, 32)
        tile[r * 32 : r * 32 + 32, :] = rows
        near[r * 16 : r * 16 + 16, :] = rows[:16]
        far[r * 16 : r * 16 + 16, :] = rows[16:]


def round_three(tile, from_y, after, before, corner, other, planes, speeds, state, msg, a, b, k, m):
    clear(a, b, -16, 48)
    load_right(a, b, tile, from_y, (after, before), (corner, other))
    for r in range(ROWS):
        k[r, Z0 - 16 : Z0 + 48, :] = speeds[r]
    advance(a, b, k, m, planes, 2, -16, 48)
    put_out(a, b, state, msg)


def round_four(flags, state, from_y, planes, speeds, above, out, a, b, k, m):
    clear(a, b, -8, 40)
    load_left(flags, state, from_y, a, b)
    load_left_speeds(k, speeds, above)
    advance(a, b, k, m, planes, 3, -8, 40)
    for p in range(4):
        turned = jnp.concatenate([a[4 * p + q, Z0 : Z0 + TZ, :] for q in range(4)], axis=0).T
        for g in range(4):
            out[pl.ds(4 * g + p, 16, stride=16), :] = turned[32 + 16 * g : 48 + 16 * g]


def deliver_kernel(flags, got, out):
    group = lane_group(16)
    for x in range(4):
        parts = []
        for zs in range(4):
            rows = [
                got[source_of(flags, ys, zs), pl.ds(x, 4, stride=4), :] for ys in range(4)
            ]
            parts.append(jnp.concatenate(rows, axis=0))
        for q in range(4):
            piece = None
            for zs in range(4):
                turn = (32 * (zs - q)) % 128
                moved = parts[zs] if turn == 0 else pltpu.roll(parts[zs], turn, 1)
                piece = moved if piece is None else jnp.where(group == zs, moved, piece)
            out[x, pl.ds(q, 16, stride=4), :] = piece


def call(kernel, outs, *args, flags=None, scratch=False, cost=2_000_000):
    shapes = [jax.ShapeDtypeStruct(s, F32) for s in outs]
    specs = [VM] * len(args)
    if flags is not None:
        args = (flags,) + args
        specs = [SM] + specs
    return pl.pallas_call(
        kernel,
        out_shape=shapes,
        in_specs=specs,
        out_specs=[VM] * len(outs),
        scratch_shapes=(
            [pltpu.VMEM((ROWS, WZ, 128), F32)] * 4 * scratch
            + [pltpu.VMEM((8, ROWS * 4, 128), F32)] * (kernel is round_one)
        ),
        compiler_params=pltpu.CompilerParams(vmem_limit_bytes=48 * 1024 * 1024),
        cost_estimate=pl.CostEstimate(flops=cost, bytes_accessed=1_000_000, transcendentals=0),
    )(*args)


def local(
    traces,
    receiver_cell,
    weight_class,
    weight_table,
    obstacle_top,
    obstacle_thick,
    courant,
    p_now,
    p_prev,
):
    zh, yc, zl, core, gz = (lax.axis_index(a) for a in AXES)
    gy = zl * 2 + core
    flip_z = gz % 2
    ty = gy * 4 + jnp.where(core == 0, yc - zl, zl - yc) % 4
    place = jnp.stack([zl, core, flip_z, gz * 128, 7 - 2 * gz - core]).astype(jnp.int32)
    packed = pl.pallas_call(
        pack_kernel,
        out_shape=jax.ShapeDtypeStruct((16, MSG_ROWS, 128), F32),
        in_specs=[SM, SM] + [VM] * 8,
        out_specs=VM,
        scratch_shapes=[pltpu.VMEM((4, 64, 128), F32), pltpu.VMEM((8, 4, 512), F32)],
        name="pack",
    )(
        place, weight_table, p_now, p_prev, courant, obstacle_top, obstacle_thick,
        traces.T, receiver_cell.reshape(4, 128), weight_class.reshape(4, 128),
    )
    got = lax.all_to_all(packed, ("zh", "yc"), 0, 0, tiled=True).reshape(16 * MSG_ROWS, 128)

    def moved(array, dy, dz):
        return lax.ppermute(array, AXES, pairs_along(dy, dz))


    def around(near, far):
        after = moved(near, 0, 1)
        before = moved(far, 0, -1)
        corner = moved(after, 1, 0)
        other = moved(before, 1, 0)
        return after, before, corner, other

    tile, near, far = call(unpack_kernel, [(768, 128), (384, 128), (384, 128)], got)
    from_y = moved(tile, 1, 0)
    firsts = [
        zl * 128 - 8 * (gz % 2) + 16 * ((yc - zl) % 4),
        zl * 128 - 8 * (gz % 2) + 64 + 16 * ((zl - yc) % 4),
    ]
    firsts = [jnp.where(core == 0, *firsts), jnp.where(core == 0, *firsts[::-1])]
    works = jnp.stack([zh == 0] + firsts + [core]).astype(jnp.int32)
    planes, mine, others = call(
        source_kernel, [(8, ROWS * 4, 128), (ROWS * 4, 128), (ROWS * 4, 128)],
        got, flags=works, cost=20_000_000,
    )
    others = lax.ppermute(others, "core", [(0, 1), (1, 0)])
    planes = lax.all_to_all(planes, ("core", "gz"), 0, 0, tiled=True)
    edges = around(near, far)
    surface = jnp.stack([core, gz == 0]).astype(jnp.int32)
    first_y = (ty == 0).astype(jnp.int32)[None]

    state, msg, speeds = call(
        round_one, [(2 * ROWS, 48, 128), (960, 128), (ROWS, 64, 128)],
        tile, from_y, *edges, mine, others, flags=surface, scratch=True,
    )
    above = moved(msg, -1, 0)
    tile, near, far = call(
        round_two, [(512, 128), (256, 128), (256, 128)],
        state, above, planes, speeds, flags=first_y, scratch=True,
    )
    from_y = moved(tile, 1, 0)
    edges = around(near, far)
    state, msg = call(
        round_three, [(2 * ROWS, 48, 128), (768, 128)],
        tile, from_y, *edges, planes, speeds, scratch=True,
    )
    (out,) = call(
        round_four, [(256, 128)],
        state, moved(msg, -1, 0), planes, speeds, above, flags=first_y, scratch=True,
    )
    out = lax.all_to_all(out.reshape(16, 16, 128), ("zh", "yc"), 0, 0, tiled=True)
    (wavefield,) = call(deliver_kernel, [(4, 64, 128)], out, flags=place)
    return wavefield


def solution(mesh):
    fine = Mesh(mesh.devices.reshape(SIZES), AXES)
    gx, gy, gz = ("zh", "yc"), ("zl", "core"), "gz"
    placed = (
        P(gx, None),
        P(gx),
        P(gx),
        P(),
        P(gx, gy),
        P(gx, gy),
        P(gx, gy, gz),
        P(gx, gy, gz),
        P(gx, gy, gz),
    )

    return jax.shard_map(
        local, mesh=fine, in_specs=placed, out_specs=P(gx, gy, gz), check_vma=False
    )
```
